128 devices in a mesh: req: 4 (over y), exp: 32 (over z, x, core).
Axes of the slice: x: 4, y: 4, z: 4, core: 2. Of those that a mesh axis runs over, the one named last changes fastest.
Arguments:
- hidden: bfloat16 [8, 2048, 2048], P('req', 'exp'), may hold values from -6 to 6
- q_new: bfloat16 [8, 16, 2048, 128], P('req', None, 'exp'), may hold values from -480 to 480
- k_new: bfloat16 [8, 16, 2048, 128], P('req', None, 'exp'), may hold values from -6 to 6
- v_new: bfloat16 [8, 16, 2048, 128], P('req', None, 'exp'), may hold values from -6 to 6
- routes: int32 [8, 2048, 6], P('req', 'exp'), may hold values from 0 to 63, all different within a row; in each aligned block of 64 rows (0 to 63, 64 to 127, ..., all dimensions but the last counted through in order) at most 8 rows name the same one
- slot_request: int32 [8], replicated, may hold values from 0 to 7, each once
- lengths: int32 [8], replicated, may hold values from 5 to 16384, as said below
- cycle_cache: bfloat16 [128, 2, 4096, 128], P(('req', 'exp')), may hold values from -6 to 6
- sink_cache: bfloat16 [128, 2, 4, 128], P(('req', 'exp')), may hold values from -6 to 6
- w_out: bfloat16 [2048, 2048], replicated, may hold values from -0.125 to 0.125
- norm_gain: float32 [2048], replicated, may hold values from 0.5 to 1.5
- router: bfloat16 [2048, 64], replicated, may hold values from -0.125 to 0.125
- w_gate: bfloat16 [2048, 90112], P(None, ('req', 'exp')), may hold values from -0.125 to 0.125
- w_up: bfloat16 [2048, 90112], P(None, ('req', 'exp')), may hold values from -0.125 to 0.125
- w_down: bfloat16 [90112, 2048], P(('req', 'exp')), may hold values from -0.15625 to 0.15625
Outputs:
- layer_out: bfloat16 [8, 2048, 2048], P('req', 'exp')
- cycle_out: bfloat16 [128, 2, 4096, 128], P(('req', 'exp'))
The draws below stay inside these ranges and needn't reach their ends.
Inputs may be any that keep to these rules, and one draw needn't show every extreme that they name: In every aligned block of 64 rows of routes (the rows of one request on one index of exp) no expert is named by more than 8 rows, a bound that some block reaches. `slot_request`: each request once. `lengths`: some slot has exactly 16384 cached tokens, and some other fewer than 2048.
All inputs are finite; a program needn't handle non-finite values.
Results may differ from the reference program's by a relative error of at most 0.014.
The reference program's roundings to bfloat16 on the way count: a program that leaves them out, or rounds other values in their place, can miss the bound.
Values may be sent and summed in bfloat16 or wider, within the bound.
No kernel may reach another device: no remote copies, remote signals or barrier semaphores. Data moves between devices by JAX's collectives and lax.ppermute only.
A program may use at most 192 MiB of HBM per device.

```python
import math
import jax
import jax.numpy as jnp
import numpy as np
from jax import lax

D = 2048
HEADS = 16
HD = 128
EXPERTS = 64
FF = 1408
TOP = 6
QD = 64
WINDOW = 4096
SINKS = 4
CTX = 16384
SPLIT = 2
QLEN = 2048
REQS = 8
MOST = 8
N_EXP = 32


def draw_q_new(key, part):
    normal_key = jax.random.fold_in(key, 0)
    values = 2.0 * jnp.clip(jax.random.normal(normal_key, (REQS, HEADS, QLEN, HD), jnp.float32), -6.0, 6.0)
    return values.astype(jnp.bfloat16)


def draw_lengths(key, part):
    key_list = jax.random.split(key, 4)
    values = jax.random.randint(key_list[0], (REQS,), SINKS + 1, CTX + 1)
    longest = jax.random.randint(key_list[1], (), 0, REQS)
    shorter = (longest + 1 + jax.random.randint(key_list[2], (), 0, REQS - 1)) % REQS
    briefest = jax.random.randint(key_list[3], (), SINKS + 1, WINDOW // 2)
    places = jnp.arange(REQS)
    values = jnp.where(places == longest, CTX, values)
    values = jnp.where(places == shorter, briefest, values)
    return values.astype(jnp.int32)


def block_levels(stream_key, extent, cuts, least, largest):
    def one(position, parts):
        draws = jax.random.uniform(jax.random.fold_in(jax.random.fold_in(stream_key, 6), position), (parts,), jnp.float32, least / len(cuts), largest / len(cuts))
        return jnp.repeat(jnp.exp(draws), extent[position] // parts).reshape((-1,) + (1,) * (len(extent) - position - 1))

    gain = one(*cuts[0])
    for cut in cuts[1:]:
        gain = gain * one(*cut)
    return gain


def assign_block(own_key, own, number, rows, count, top, reach, slope):
    ranking = jax.random.permutation(own_key, count)
    crowded, ordinary = shares(count, rows * top, reach, slope, True), shares(count, rows * top, reach, slope, False)
    places = jnp.arange(count)

    def named(tallies, turn):
        used = int((tallies > 0).sum())
        fixed = max(1, used // 4)
        passed = fixed + (places - fixed + turn * (used - fixed)) % max(1, count - fixed)
        return jnp.zeros((count,), jnp.int32).at[ranking[jnp.where(places < fixed, places, passed)]].set(jnp.asarray(tallies, jnp.int32))

    tallies = jnp.where(number % 4 == 0, named(crowded, number // 4), named(ordinary, number - number // 4 - 1))
    mixed = jax.random.permutation(jax.random.fold_in(own, 3), count)
    giver, receiver = mixed[0:count // 2 * 2:2], mixed[1:count // 2 * 2:2]
    margin = jnp.minimum(tallies[giver] - 1, reach - tallies[receiver]) // 2
    margin = jnp.where((giver == ranking[0]) | (receiver == ranking[0]) | (tallies[receiver] == 0), 0, jnp.maximum(margin, 0))
    passed = jax.random.randint(jax.random.fold_in(own, 4), (count // 2,), 0, 1 << 20) % (margin + 1)
    tallies = tallies.at[giver].add(-passed).at[receiver].add(passed)
    items = jnp.searchsorted(jnp.cumsum(tallies), jnp.arange(rows * top), side="right").astype(jnp.int32)
    listing = items.reshape(top, rows).T
    listing = listing[jax.random.permutation(jax.random.fold_in(own, 1), rows)]
    turn = jax.random.randint(jax.random.fold_in(own, 2), (rows, 1), 0, top)
    return jnp.take_along_axis(listing, (jnp.arange(top)[None, :] + turn) % top, axis=1)


def shares(number_of, total, reach, skew, full):
    loads = [(1 << 20) // math.isqrt(rank ** skew) + 1 for rank in range(1, number_of + 1)]
    largest = reach if full else min(reach, max(-(-total // number_of), total * loads[0] // sum(loads)))
    least = 1 if total - largest >= number_of - 1 else 0
    counts, spare = [largest] + [least] * (number_of - 1), total - largest - least * (number_of - 1)
    while spare > 0:
        free = [i for i in range(1, number_of) if counts[i] < largest] or [i for i in range(1, number_of) if counts[i] < reach]
        mass, left = sum([loads[i] for i in free]), spare
        for i in free:
            addition = min(reach - counts[i], max(1, left * loads[i] // mass), spare)
            counts[i] = counts[i] + addition
            spare = spare - addition
    return np.array(counts)


def scatter_about(key, dims, deviation, limit, cuts=(), kind=jnp.bfloat16):
    result = deviation * jax.random.normal(key, dims, jnp.float32)
    if cuts:
        result = result * block_levels(key, dims, cuts, -0.22, 0.18)
    return jnp.clip(result, -limit, limit).astype(kind)


def setup_inputs(seed: int = 0) -> dict:
    splits = jax.random.split(jax.random.key(seed), 16)
    hidden = scatter_about(splits[0], (REQS, QLEN, D), 1.0, 6.0, ((0, 4), (1, 32)))
    q_new = draw_q_new(jax.random.fold_in(splits[15], 71), 0)
    k_new = scatter_about(splits[2], (REQS, HEADS, QLEN, HD), 1.0, 6.0, ((0, 4), (2, 32)))
    v_new = scatter_about(splits[3], (REQS, HEADS, QLEN, HD), 1.0, 6.0, ((0, 4), (2, 32)))
    routes_keys = jax.random.split(jax.random.fold_in(splits[4], 1), REQS * QLEN // QD)
    routes_turns = jax.random.permutation(jax.random.fold_in(splits[4], 3), REQS * QLEN // QD)
    routes = jax.vmap(lambda own, number: assign_block(jax.random.fold_in(splits[4], 2), own, number, QD, EXPERTS, TOP, MOST, 2))(routes_keys, routes_turns).reshape((REQS, QLEN, TOP))
    slot_request = jax.random.permutation(splits[5], REQS).astype(jnp.int32)
    lengths = draw_lengths(jax.random.fold_in(splits[15], 71), 0)
    cycle_cache = scatter_about(splits[7], (REQS * HEADS, 2, WINDOW, HD), 1.0, 6.0, ((0, 128),))
    sink_cache = scatter_about(splits[8], (REQS * HEADS, 2, SINKS, HD), 1.0, 6.0, ((0, 128),))
    w_out = scatter_about(splits[9], (D, D), D ** -0.5, 0.125)
    norm_gain = jnp.clip(1.0 + 0.1 * jax.random.normal(splits[10], (D,), jnp.float32), 0.5, 1.5)
    router = scatter_about(splits[11], (D, EXPERTS), D ** -0.5, 0.125)
    w_gate = scatter_about(splits[12], (D, EXPERTS * FF), D ** -0.5, 0.125, ((1, 128),))
    w_up = scatter_about(splits[13], (D, EXPERTS * FF), D ** -0.5, 0.125, ((1, 128),))
    w_down = scatter_about(splits[14], (EXPERTS * FF, D), FF ** -0.5, 0.15625, ((0, 128),))
    return dict(hidden=hidden, q_new=q_new, k_new=k_new, v_new=v_new, routes=routes, slot_request=slot_request, lengths=lengths, cycle_cache=cycle_cache, sink_cache=sink_cache, w_out=w_out, norm_gain=norm_gain, router=router, w_gate=w_gate, w_up=w_up, w_down=w_down)


def rotate(vectors, positions):
    half_width = vectors.shape[-1] // 2
    frequency = 10000.0 ** (-2.0 * jnp.arange(half_width, dtype=jnp.float32) / vectors.shape[-1])
    angles = positions.astype(jnp.float32)[:, None] * frequency[None, :]
    cosine = jnp.cos(angles)
    sine_part = jnp.sin(angles)
    low_half = vectors[..., :half_width]
    high_half = vectors[..., half_width:]
    return jnp.concatenate([low_half * cosine - high_half * sine_part, high_half * cosine + low_half * sine_part], axis=-1)

def attend_pair(query_rows, key_new, value_new, cycle_pair, sink_pair, length):
    positions = length + jnp.arange(QLEN, dtype=jnp.int32)
    q_rot = rotate(query_rows.astype(jnp.float32), positions).astype(jnp.bfloat16)
    k_rot = rotate(key_new.astype(jnp.float32), positions).astype(jnp.bfloat16)
    cycle_slots = jnp.arange(WINDOW, dtype=jnp.int32)
    cycle_positions = cycle_slots + WINDOW * ((length - 1 - cycle_slots) // WINDOW)
    key_rows = jnp.concatenate([cycle_pair[0], k_rot], 0)
    value_rows = jnp.concatenate([cycle_pair[1], value_new], 0)
    key_positions = jnp.concatenate([cycle_positions, positions], 0)
    visible = (key_positions[None, :] >= 0) & (key_positions[None, :] <= positions[:, None]) & (key_positions[None, :] > positions[:, None] - WINDOW)
    score_scale = HD ** (-0.5)
    scores = jnp.dot(q_rot, key_rows.T, preferred_element_type=jnp.float32) * score_scale
    scores = jnp.where(visible, scores, -jnp.inf)
    sink_scores = jnp.dot(q_rot, sink_pair[0].T, preferred_element_type=jnp.float32) * score_scale
    sink_visible = jnp.arange(SINKS, dtype=jnp.int32)[None, :] <= positions[:, None] - WINDOW
    sink_scores = jnp.where(sink_visible, sink_scores, -jnp.inf)
    highest = jnp.maximum(lax.optimization_barrier(jnp.max(scores, axis=1)), lax.optimization_barrier(jnp.max(sink_scores, axis=1)))[:, None]
    weights = jnp.exp(scores - highest)
    sink_weights = jnp.exp(sink_scores - highest)
    denominator = lax.optimization_barrier(jnp.sum(weights, axis=1)) + lax.optimization_barrier(jnp.sum(sink_weights, axis=1))
    blended = jnp.dot(weights.astype(jnp.bfloat16), value_rows, preferred_element_type=jnp.float32)
    blended = blended + jnp.dot(sink_weights.astype(jnp.bfloat16), sink_pair[1], preferred_element_type=jnp.float32)
    context = (blended / denominator[:, None]).astype(jnp.bfloat16)
    new_slots = positions % WINDOW
    updated = jnp.stack([cycle_pair[0].at[new_slots].set(k_rot), cycle_pair[1].at[new_slots].set(value_new)])
    return (context, updated)

def reference(hidden, q_new, k_new, v_new, routes, slot_request, lengths, cycle_cache, sink_cache, w_out, norm_gain, router, w_gate, w_up, w_down):
    pair_count = REQS * HEADS
    query_all = jnp.take(q_new, slot_request, axis=0).reshape(pair_count, QLEN, HD)
    key_all = jnp.take(k_new, slot_request, axis=0).reshape(pair_count, QLEN, HD)
    value_all = jnp.take(v_new, slot_request, axis=0).reshape(pair_count, QLEN, HD)
    pair_lengths = jnp.repeat(lengths, HEADS)
    context, cycle_out = lax.map(lambda packed: attend_pair(*packed), (query_all, key_all, value_all, cycle_cache, sink_cache, pair_lengths))
    context = context.reshape(REQS, HEADS, QLEN, HD)
    projected = jnp.einsum('shqd,hde->sqe', context.astype(jnp.float32), w_out.reshape(HEADS, HD, D).astype(jnp.float32))
    residual = jnp.take(hidden, slot_request, axis=0).astype(jnp.float32) + projected
    inverse = lax.rsqrt(lax.optimization_barrier(jnp.mean(residual * residual, axis=-1, keepdims=True)) + 1e-06)
    normed = (residual * inverse * norm_gain.astype(jnp.float32)).astype(jnp.bfloat16).reshape(REQS * QLEN, D)
    logits = jnp.dot(normed, router, preferred_element_type=jnp.float32)
    chosen = jnp.take(routes, slot_request, axis=0).reshape(REQS * QLEN, TOP)
    gates = jax.nn.softmax(jnp.take_along_axis(logits, chosen, axis=1), axis=-1)
    capacity = REQS * N_EXP * MOST
    half_units = FF // SPLIT

    def per_expert(running, expert):
        matched = chosen == expert
        member = jnp.any(matched, axis=1)
        weight_row = lax.optimization_barrier(jnp.sum(jnp.where(matched, gates, 0.0), axis=1))
        indices = jnp.nonzero(member, size=capacity, fill_value=0)[0].astype(jnp.int32)
        filled = jnp.arange(capacity, dtype=jnp.int32) < jnp.sum(member.astype(jnp.int32))
        selected = jnp.take(normed, indices, axis=0)
        gate_cols = lax.dynamic_slice_in_dim(w_gate, expert * FF, FF, 1)
        up_cols = lax.dynamic_slice_in_dim(w_up, expert * FF, FF, 1)
        down_rows = lax.dynamic_slice_in_dim(w_down, expert * FF, FF, 0)
        summed = jnp.zeros((capacity, D), jnp.float32)
        for piece_number in range(SPLIT):
            first_unit = piece_number * half_units
            gate_part = jnp.dot(selected, gate_cols[:, first_unit:first_unit + half_units], preferred_element_type=jnp.float32)
            up_part = jnp.dot(selected, up_cols[:, first_unit:first_unit + half_units], preferred_element_type=jnp.float32)
            active = (jax.nn.silu(gate_part) * up_part).astype(jnp.bfloat16)
            output_part = jnp.dot(active, down_rows[first_unit:first_unit + half_units], preferred_element_type=jnp.float32).astype(jnp.bfloat16)
            summed = summed + lax.optimization_barrier(output_part).astype(jnp.float32)
        scaled = jnp.where(filled, jnp.take(weight_row, indices), 0.0)[:, None] * summed
        return (running.at[indices].add(scaled), None)
    moe, _ = lax.scan(per_expert, jnp.zeros((REQS * QLEN, D), jnp.float32), jnp.arange(EXPERTS, dtype=jnp.int32))
    layer_out = (residual.reshape(REQS * QLEN, D) + moe).astype(jnp.bfloat16).reshape(REQS, QLEN, D)
    return (layer_out, cycle_out)
```

```python
import functools
import math

import jax
import jax.numpy as jnp
from jax import lax
from jax.experimental import pallas as pl
from jax.experimental.pallas import tpu as pltpu
from jax.sharding import PartitionSpec as P

SPLIT = 2
MOST = 8
BLOCK = 512
SINK_PAD = 128
GRAIN = 16


def rotary_tables(length, count, width):
    half_width = width // 2
    frequency = 10000.0 ** (-2.0 * jnp.arange(half_width, dtype=jnp.float32) / width)
    positions = length + jnp.arange(count, dtype=jnp.int32)
    angles = positions.astype(jnp.float32)[:, None] * frequency[None, :]
    cosine = jnp.cos(angles)
    sine = jnp.sin(angles)
    return (
        jnp.concatenate([cosine, cosine], axis=1),
        jnp.concatenate([-sine, sine], axis=1),
    )


def attention_kernel(
    info, arrived, cache, sink, cosine, sine, context, cache_out, k_rot, v_new, scores, shifted, top_acc, sum_acc, out_acc
):
    step = pl.program_id(0)
    length = info[1]
    window = cache.shape[2]
    rows = arrived.shape[2] // 3
    seq_len = arrived.shape[1] * rows
    width = arrived.shape[3]
    chunks = BLOCK // rows
    turn = lax.rem(length, window)

    def rotated(first_chunk, row_from, kind):
        raw = arrived[0, pl.ds(first_chunk, chunks), kind * rows : (kind + 1) * rows, :]
        raw = raw.reshape(BLOCK, width).astype(jnp.float32)
        cos_rows = cosine[pl.ds(row_from, BLOCK), :]
        sin_rows = sine[pl.ds(row_from, BLOCK), :]
        return raw * cos_rows + pltpu.roll(raw, width // 2, 1) * sin_rows

    @pl.when(step == 0)
    def _():
        for part in range(seq_len // BLOCK):
            k_rot[part * BLOCK : (part + 1) * BLOCK, :] = rotated(
                part * chunks, part * BLOCK, 1
            ).astype(jnp.bfloat16)
            v_new[part * BLOCK : (part + 1) * BLOCK, :] = arrived[
                0, part * chunks : (part + 1) * chunks, 2 * rows : 3 * rows, :
            ].reshape(BLOCK, width)
        shift = lax.rem(turn, GRAIN)
        base = turn - shift
        last = lax.rem(base + seq_len, window)
        for kind, fresh in ((0, k_rot), (1, v_new)):
            cache_out[0, kind] = cache[0, kind]
            shifted[0:GRAIN, :] = cache[
                0, kind, pl.ds(pl.multiple_of(base, GRAIN), GRAIN), :
            ].astype(jnp.float32)
            shifted[seq_len : seq_len + GRAIN, :] = cache[
                0, kind, pl.ds(pl.multiple_of(last, GRAIN), GRAIN), :
            ].astype(jnp.float32)
            shifted[pl.ds(shift, seq_len), :] = fresh[...].astype(jnp.float32)

            def place(index, carry):
                target = pl.multiple_of(lax.rem(base + index * GRAIN, window), GRAIN)
                cache_out[0, kind, pl.ds(target, GRAIN), :] = shifted[
                    pl.ds(pl.multiple_of(index * GRAIN, GRAIN), GRAIN), :
                ].astype(jnp.bfloat16)
                return carry

            lax.fori_loop(0, seq_len // GRAIN + 1, place, 0)

    first_row = step * BLOCK
    query = rotated(step * chunks, first_row, 0).astype(jnp.bfloat16)
    row_ids = first_row + lax.broadcasted_iota(jnp.int32, (BLOCK, 1), 0)
    cycle_blocks = window // BLOCK
    new_blocks = seq_len // BLOCK
    sink_block = cycle_blocks + new_blocks
    contract_last = (((1,), (1,)), ((), ()))

    def score(keys):
        return lax.dot_general(query, keys, contract_last, preferred_element_type=jnp.float32)

    def note(block, values):
        best = top_acc[...]
        for lane in range(values.shape[1] // 128):
            best = jnp.maximum(best, values[:, lane * 128 : (lane + 1) * 128])
        top_acc[...] = best
        if values.shape[1] == BLOCK:
            scores[block] = values
        else:
            scores[block, :, 0 : values.shape[1]] = values

    lowest = jnp.float32(-jnp.inf)
    top_acc[...] = jnp.full_like(top_acc, -jnp.inf)

    def order_from(block):
        return lax.rem(block * BLOCK - turn + window, window)

    def cycle_seen(block):
        end = order_from(block) + BLOCK - 1
        return (end > first_row) & (end >= window - length)

    def score_cycle(block, carry):
        start = order_from(block)
        whole = (
            (start + BLOCK <= window)
            & (start > first_row + BLOCK - 1)
            & (start >= window - length)
        )
        keys_at = pl.ds(pl.multiple_of(block * BLOCK, BLOCK), BLOCK)

        @pl.when(whole)
        def _():
            note(block, score(cache[0, 0, keys_at, :]))

        @pl.when(cycle_seen(block) & jnp.logical_not(whole))
        def _():
            order = lax.rem(start + lax.broadcasted_iota(jnp.int32, (1, BLOCK), 1), window)
            order = jnp.where(order >= window - length, order, -1)
            note(block, jnp.where(order > row_ids, score(cache[0, 0, keys_at, :]), lowest))

        return carry

    lax.fori_loop(0, cycle_blocks, score_cycle, 0)

    def score_new(block, carry):
        keys_at = pl.ds(pl.multiple_of(block * BLOCK, BLOCK), BLOCK)
        note(cycle_blocks + block, score(k_rot[keys_at, :]))
        return carry

    lax.fori_loop(0, step, score_new, 0)
    own_at = pl.ds(pl.multiple_of(first_row, BLOCK), BLOCK)
    columns = first_row + lax.broadcasted_iota(jnp.int32, (1, BLOCK), 1)
    note(cycle_blocks + step, jnp.where(columns <= row_ids, score(k_rot[own_at, :]), lowest))
    sink_columns = lax.broadcasted_iota(jnp.int32, (1, SINK_PAD), 1)
    sink_columns = jnp.where(sink_columns < info[2], sink_columns, window + 2 * seq_len + length)
    note(
        sink_block,
        jnp.where(sink_columns <= length + row_ids - window, score(sink[0, 0]), lowest),
    )

    top = jnp.max(top_acc[...], axis=1, keepdims=True)
    factor = jnp.float32(width ** (-0.5) * math.log2(math.e))

    def weights_of(values):
        return jnp.exp2((values - top) * factor)

    def add_up(weights, values):
        total = sum_acc[...]
        for lane in range(weights.shape[1] // 128):
            total = total + weights[:, lane * 128 : (lane + 1) * 128]
        sum_acc[...] = total
        out_acc[...] += jnp.dot(
            weights.astype(jnp.bfloat16), values, preferred_element_type=jnp.float32
        )

    sink_weights = weights_of(scores[sink_block, :, 0:SINK_PAD])
    sum_acc[...] = sink_weights
    out_acc[...] = jnp.dot(
        sink_weights.astype(jnp.bfloat16), sink[0, 1], preferred_element_type=jnp.float32
    )

    def blend_cycle(block, carry):
        @pl.when(cycle_seen(block))
        def _():
            add_up(
                weights_of(scores[block]),
                cache[0, 1, pl.ds(pl.multiple_of(block * BLOCK, BLOCK), BLOCK), :],
            )

        return carry

    lax.fori_loop(0, cycle_blocks, blend_cycle, 0)

    def blend_new(block, carry):
        add_up(
            weights_of(scores[cycle_blocks + block]),
            v_new[pl.ds(pl.multiple_of(block * BLOCK, BLOCK), BLOCK), :],
        )
        return carry

    lax.fori_loop(0, step + 1, blend_new, 0)
    total = jnp.sum(sum_acc[...], axis=1, keepdims=True)
    context[...] = (out_acc[...] / total).astype(jnp.bfloat16)


def attend(info, arrived, cache, sink, cosine, sine, interpret=False):
    groups, senders, rows3, width = arrived.shape
    seq_len = senders * (rows3 // 3)
    window = cache.shape[2]
    block_count = window // BLOCK + seq_len // BLOCK + 1
    once = pl.Buffered(1)
    return pl.pallas_call(
        attention_kernel,
        grid_spec=pltpu.PrefetchScalarGridSpec(
            num_scalar_prefetch=1,
            grid=(seq_len // BLOCK,),
            in_specs=[
                pl.BlockSpec((1, senders, rows3, width), lambda i, info: (info[0], 0, 0, 0), pipeline_mode=once),
                pl.BlockSpec((1, 2, window, width), lambda i, info: (0, 0, 0, 0), pipeline_mode=once),
                pl.BlockSpec((1, 2, SINK_PAD, width), lambda i, info: (0, 0, 0, 0), pipeline_mode=once),
                pl.BlockSpec((seq_len, width), lambda i, info: (0, 0), pipeline_mode=once),
                pl.BlockSpec((seq_len, width), lambda i, info: (0, 0), pipeline_mode=once),
            ],
            out_specs=[
                pl.BlockSpec((BLOCK, width), lambda i, info: (i, 0)),
                pl.BlockSpec((1, 2, window, width), lambda i, info: (0, 0, 0, 0), pipeline_mode=once),
            ],
            scratch_shapes=[
                pltpu.VMEM((seq_len, width), jnp.bfloat16),
                pltpu.VMEM((seq_len, width), jnp.bfloat16),
                pltpu.VMEM((block_count, BLOCK, BLOCK), jnp.float32),
                pltpu.VMEM((seq_len + GRAIN, width), jnp.float32),
                pltpu.VMEM((BLOCK, 128), jnp.float32),
                pltpu.VMEM((BLOCK, 128), jnp.float32),
                pltpu.VMEM((BLOCK, width), jnp.float32),
            ],
        ),
        out_shape=[
            jax.ShapeDtypeStruct((seq_len, width), jnp.bfloat16),
            jax.ShapeDtypeStruct(cache.shape, jnp.bfloat16),
        ],
        compiler_params=pltpu.CompilerParams(
            dimension_semantics=("arbitrary",), vmem_limit_bytes=48 << 20
        ),
        interpret=interpret,
        name="attend",
    )(info, arrived, cache, sink, cosine, sine)


def on_device(
    hidden,
    q_new,
    k_new,
    v_new,
    routes,
    slot_request,
    lengths,
    cycle_cache,
    sink_cache,
    w_out,
    norm_gain,
    router,
    w_gate,
    w_up,
    w_down,
):
    group_width = lax.axis_size("exp")
    group_count = lax.axis_size("req")
    devices_all = group_count * group_width
    group_index = lax.axis_index("req")
    member_index = lax.axis_index("exp")
    slots_here, local_rows, model_width = hidden.shape
    head_count = q_new.shape[1]
    head_dim = q_new.shape[3]
    experts_all = router.shape[1]
    slots_all = slot_request.shape[0]
    seq_len = local_rows * group_width
    tokens = slots_here * local_rows

    held = jnp.clip(slot_request - group_index * slots_here, 0, slots_here - 1)
    source_group = slot_request // slots_here

    def laid_out(part):
        chosen = part[0][None]
        for index in range(1, slots_here):
            flag = (held == index).reshape((slots_all,) + (1,) * (part.ndim - 1))
            chosen = jnp.where(flag, part[index][None], chosen)
        return chosen

    outgoing = laid_out(jnp.concatenate([q_new, k_new, v_new], axis=2))
    outgoing = outgoing.reshape(devices_all, 3 * local_rows, head_dim)
    arrived = lax.all_to_all(outgoing, ("req", "exp"), split_axis=0, concat_axis=0, tiled=True)
    arrived = arrived.reshape(group_count, group_width, 3 * local_rows, head_dim)

    routes_wide = jnp.pad(
        routes.astype(jnp.bfloat16), ((0, 0), (0, 0), (0, 128 - routes.shape[2]))
    )
    states = laid_out(jnp.concatenate([hidden, routes_wide], axis=2))
    states = states.reshape(group_count, tokens, model_width + 128)
    states = lax.all_to_all(states, "req", split_axis=0, concat_axis=0, tiled=True)
    states = states.reshape(group_count, slots_here, local_rows, model_width + 128)
    own_sources = lax.dynamic_slice_in_dim(
        source_group, group_index * slots_here, slots_here
    )
    states = jnp.concatenate(
        [
            lax.dynamic_index_in_dim(states[:, slot], own_sources[slot], 0, keepdims=False)
            for slot in range(slots_here)
        ],
        0,
    )
    hidden_sel = states[:, :model_width]
    route_sel = states[:, model_width : model_width + routes.shape[2]].astype(jnp.int32)

    slot_here = group_index * slots_here + member_index // head_count
    length = lax.dynamic_index_in_dim(lengths, slot_here, 0, keepdims=False)
    source = lax.dynamic_index_in_dim(source_group, slot_here, 0, keepdims=False)
    cosine, sine = rotary_tables(length, seq_len, head_dim)
    sink_count = sink_cache.shape[2]
    sink_padded = jnp.pad(sink_cache, ((0, 0), (0, 0), (0, SINK_PAD - sink_count), (0, 0)))
    info = jnp.stack([source, length, jnp.int32(sink_count)]).astype(jnp.int32)
    context, cycle_out = attend(info, arrived, cycle_cache, sink_padded, cosine, sine)

    context_rows = lax.all_to_all(
        context.reshape(group_width, local_rows, head_dim),
        "exp",
        split_axis=0,
        concat_axis=0,
        tiled=True,
    ).reshape(slots_here, head_count, local_rows, head_dim)
    context_rows = jnp.transpose(context_rows, (0, 2, 1, 3)).reshape(tokens, head_count * head_dim)
    projected = jnp.dot(context_rows, w_out, preferred_element_type=jnp.float32)
    residual = hidden_sel.astype(jnp.float32) + projected
    inverse = lax.rsqrt(jnp.mean(residual * residual, axis=-1, keepdims=True) + 1e-06)
    normed = (residual * inverse * norm_gain).astype(jnp.bfloat16)

    logits = lax.dot_general(
        router, normed, (((0,), (1,)), ((), ())), preferred_element_type=jnp.float32
    )
    expert_ids = jnp.arange(experts_all, dtype=jnp.int32)
    named = jnp.any(route_sel.T[None] == expert_ids[:, None, None], axis=1)
    token_ids = jnp.arange(tokens, dtype=jnp.int32)
    token_slot = token_ids // local_rows
    before = (token_ids[:, None] < token_ids[None, :]) & (
        token_slot[:, None] == token_slot[None, :]
    )
    ranks = jnp.dot(
        named.astype(jnp.bfloat16), before.astype(jnp.bfloat16), preferred_element_type=jnp.float32
    ).astype(jnp.int32)
    seats = jnp.arange(slots_here * MOST, dtype=jnp.int32)
    seated = named[:, None, :] & (
        token_slot[None, None, :] * MOST + ranks[:, None, :] == seats[None, :, None]
    )
    masked = jnp.where(named, logits, -jnp.inf)
    raised = jnp.exp(masked - jnp.max(masked, axis=0, keepdims=True))
    gates = raised / jnp.sum(raised, axis=0, keepdims=True)

    seats_all = experts_all * slots_here * MOST
    seating = seated.reshape(seats_all, tokens).astype(jnp.bfloat16)
    buffer = jnp.dot(seating, normed, preferred_element_type=jnp.float32).astype(jnp.bfloat16)
    received = lax.all_to_all(
        buffer.reshape(devices_all, MOST, model_width),
        ("req", "exp"),
        split_axis=0,
        concat_axis=0,
        tiled=True,
    ).reshape(devices_all * MOST, model_width)
    swap = [(index, index ^ 1) for index in range(group_width)]

    def piece(rows):
        gate_part = jnp.dot(rows, w_gate, preferred_element_type=jnp.float32)
        up_part = jnp.dot(rows, w_up, preferred_element_type=jnp.float32)
        active = (jax.nn.silu(gate_part) * up_part).astype(jnp.bfloat16)
        return jnp.dot(active, w_down, preferred_element_type=jnp.float32).astype(jnp.bfloat16)

    other_rows = lax.ppermute(received, "exp", swap)
    own_piece = piece(received)
    other_piece = lax.ppermute(piece(other_rows), "exp", swap)
    summed = (own_piece.astype(jnp.float32) + other_piece.astype(jnp.float32)).astype(jnp.bfloat16)
    returned = lax.all_to_all(
        summed.reshape(devices_all, MOST, model_width),
        ("req", "exp"),
        split_axis=0,
        concat_axis=0,
        tiled=True,
    ).reshape(seats_all, model_width)

    shares = jnp.where(seated, gates[:, None, :], 0.0).reshape(seats_all, tokens)
    coarse = lax.reduce_precision(shares, 8, 7)
    fine = (shares - coarse).astype(jnp.bfloat16)
    both = jnp.concatenate([coarse.astype(jnp.bfloat16), fine], axis=1)
    moe = lax.dot_general(
        both, returned, (((0,), (0,)), ((), ())), preferred_element_type=jnp.float32
    )
    layer_out = (residual + (moe[:tokens] + moe[tokens:])).astype(jnp.bfloat16)
    return (layer_out.reshape(slots_here, local_rows, model_width), cycle_out)


def solution(mesh):
    in_specs = (
        P("req", "exp", None),
        P("req", None, "exp", None),
        P("req", None, "exp", None),
        P("req", None, "exp", None),
        P("req", "exp", None),
        P(),
        P(),
        P(("req", "exp"), None, None, None),
        P(("req", "exp"), None, None, None),
        P(),
        P(),
        P(),
        P(None, ("req", "exp")),
        P(None, ("req", "exp")),
        P(("req", "exp"), None),
    )
    out_specs = (P("req", "exp", None), P(("req", "exp"), None, None, None))
    return jax.shard_map(
        on_device, mesh=mesh, in_specs=in_specs, out_specs=out_specs, check_vma=False
    )
```

```python
import math

import jax
import jax.numpy as jnp
from jax import lax
from jax.experimental import pallas as pl
from jax.experimental.pallas import tpu as pltpu
from jax.sharding import PartitionSpec as P


SPLIT = 2
MOST = 8
BLOCK = 512
SINK_PAD = 128
GRAIN = 16


def rotary_tables(length, count, width):
    half_width = width // 2
    frequency = 10000.0 ** (-2.0 * jnp.arange(half_width, dtype=jnp.float32) / width)
    positions = length + jnp.arange(count, dtype=jnp.int32)
    angles = positions.astype(jnp.float32)[:, None] * frequency[None, :]
    cosine = jnp.cos(angles)
    sine = jnp.sin(angles)
    return (
        jnp.concatenate([cosine, cosine], axis=1),
        jnp.concatenate([-sine, sine], axis=1),
    )


def attention_kernel(
    info, arrived, cache, sink, cosine, sine, context, cache_out, k_rot, v_new, scores, shifted, top_acc, sum_acc, out_acc
):
    step = pl.program_id(0)
    length = info[1]
    window = cache.shape[2]
    rows = arrived.shape[2] // 3
    seq_len = arrived.shape[1] * rows
    width = arrived.shape[3]
    chunks = BLOCK // rows
    turn = lax.rem(length, window)

    def rotated(first_chunk, row_from, kind):
        raw = arrived[0, pl.ds(first_chunk, chunks), kind * rows : (kind + 1) * rows, :]
        raw = raw.reshape(BLOCK, width).astype(jnp.float32)
        cos_rows = cosine[pl.ds(row_from, BLOCK), :]
        sin_rows = sine[pl.ds(row_from, BLOCK), :]
        return raw * cos_rows + pltpu.roll(raw, width // 2, 1) * sin_rows

    @pl.when(step == 0)
    def _():
        for part in range(seq_len // BLOCK):
            k_rot[part * BLOCK : (part + 1) * BLOCK, :] = rotated(
                part * chunks, part * BLOCK, 1
            ).astype(jnp.bfloat16)
            v_new[part * BLOCK : (part + 1) * BLOCK, :] = arrived[
                0, part * chunks : (part + 1) * chunks, 2 * rows : 3 * rows, :
            ].reshape(BLOCK, width)
        shift = lax.rem(turn, GRAIN)
        base = turn - shift
        last = lax.rem(base + seq_len, window)
        for kind, fresh in ((0, k_rot), (1, v_new)):
            cache_out[0, kind] = cache[0, kind]
            shifted[0:GRAIN, :] = cache[
                0, kind, pl.ds(pl.multiple_of(base, GRAIN), GRAIN), :
            ].astype(jnp.float32)
            shifted[seq_len : seq_len + GRAIN, :] = cache[
                0, kind, pl.ds(pl.multiple_of(last, GRAIN), GRAIN), :
            ].astype(jnp.float32)
            shifted[pl.ds(shift, seq_len), :] = fresh[...].astype(jnp.float32)

            def place(index, carry):
                target = pl.multiple_of(lax.rem(base + index * GRAIN, window), GRAIN)
                cache_out[0, kind, pl.ds(target, GRAIN), :] = shifted[
                    pl.ds(pl.multiple_of(index * GRAIN, GRAIN), GRAIN), :
                ].astype(jnp.bfloat16)
                return carry

            lax.fori_loop(0, seq_len // GRAIN + 1, place, 0)

    first_row = step * BLOCK
    query = rotated(step * chunks, first_row, 0).astype(jnp.bfloat16)
    row_ids = first_row + lax.broadcasted_iota(jnp.int32, (BLOCK, 1), 0)
    cycle_blocks = window // BLOCK
    new_blocks = seq_len // BLOCK
    sink_block = cycle_blocks + new_blocks
    contract_last = (((1,), (1,)), ((), ()))

    def score(keys):
        return lax.dot_general(query, keys, contract_last, preferred_element_type=jnp.float32)

    def note(block, values):
        best = top_acc[...]
        for lane in range(values.shape[1] // 128):
            best = jnp.maximum(best, values[:, lane * 128 : (lane + 1) * 128])
        top_acc[...] = best
        if values.shape[1] == BLOCK:
            scores[block] = values
        else:
            scores[block, :, 0 : values.shape[1]] = values

    lowest = jnp.float32(-jnp.inf)
    top_acc[...] = jnp.full_like(top_acc, -jnp.inf)

    def order_from(block):
        return lax.rem(block * BLOCK - turn + window, window)

    def cycle_seen(block):
        end = order_from(block) + BLOCK - 1
        return (end > first_row) & (end >= window - length)

    def score_cycle(block, carry):
        start = order_from(block)
        whole = (
            (start + BLOCK <= window)
            & (start > first_row + BLOCK - 1)
            & (start >= window - length)
        )
        keys_at = pl.ds(pl.multiple_of(block * BLOCK, BLOCK), BLOCK)

        @pl.when(whole)
        def _():
            note(block, score(cache[0, 0, keys_at, :]))

        @pl.when(cycle_seen(block) & jnp.logical_not(whole))
        def _():
            order = lax.rem(start + lax.broadcasted_iota(jnp.int32, (1, BLOCK), 1), window)
            order = jnp.where(order >= window - length, order, -1)
            note(block, jnp.where(order > row_ids, score(cache[0, 0, keys_at, :]), lowest))

        return carry

    lax.fori_loop(0, cycle_blocks, score_cycle, 0)

    def score_new(block, carry):
        keys_at = pl.ds(pl.multiple_of(block * BLOCK, BLOCK), BLOCK)
        note(cycle_blocks + block, score(k_rot[keys_at, :]))
        return carry

    lax.fori_loop(0, step, score_new, 0)
    own_at = pl.ds(pl.multiple_of(first_row, BLOCK), BLOCK)
    columns = first_row + lax.broadcasted_iota(jnp.int32, (1, BLOCK), 1)
    note(cycle_blocks + step, jnp.where(columns <= row_ids, score(k_rot[own_at, :]), lowest))
    sink_columns = lax.broadcasted_iota(jnp.int32, (1, SINK_PAD), 1)
    sink_columns = jnp.where(sink_columns < info[2], sink_columns, window + 2 * seq_len + length)
    note(
        sink_block,
        jnp.where(sink_columns <= length + row_ids - window, score(sink[0, 0]), lowest),
    )

    top = jnp.max(top_acc[...], axis=1, keepdims=True)
    factor = jnp.float32(width ** (-0.5) * math.log2(math.e))

    def weights_of(values):
        return jnp.exp2((values - top) * factor)

    def add_up(weights, values):
        total = sum_acc[...]
        for lane in range(weights.shape[1] // 128):
            total = total + weights[:, lane * 128 : (lane + 1) * 128]
        sum_acc[...] = total
        out_acc[...] += jnp.dot(
            weights.astype(jnp.bfloat16), values, preferred_element_type=jnp.float32
        )

    sink_weights = weights_of(scores[sink_block, :, 0:SINK_PAD])
    sum_acc[...] = sink_weights
    out_acc[...] = jnp.dot(
        sink_weights.astype(jnp.bfloat16), sink[0, 1], preferred_element_type=jnp.float32
    )

    def blend_cycle(block, carry):
        @pl.when(cycle_seen(block))
        def _():
            add_up(
                weights_of(scores[block]),
                cache[0, 1, pl.ds(pl.multiple_of(block * BLOCK, BLOCK), BLOCK), :],
            )

        return carry

    lax.fori_loop(0, cycle_blocks, blend_cycle, 0)

    def blend_new(block, carry):
        add_up(
            weights_of(scores[cycle_blocks + block]),
            v_new[pl.ds(pl.multiple_of(block * BLOCK, BLOCK), BLOCK), :],
        )
        return carry

    lax.fori_loop(0, step + 1, blend_new, 0)
    total = jnp.sum(sum_acc[...], axis=1, keepdims=True)
    context[...] = (out_acc[...] / total).astype(jnp.bfloat16)


def attend(info, arrived, cache, sink, cosine, sine, interpret=False):
    _, senders, rows3, width = arrived.shape
    seq_len = senders * (rows3 // 3)
    window = cache.shape[2]
    block_count = window // BLOCK + seq_len // BLOCK + 1
    once = pl.Buffered(1)
    return pl.pallas_call(
        attention_kernel,
        grid_spec=pltpu.PrefetchScalarGridSpec(
            num_scalar_prefetch=1,
            grid=(seq_len // BLOCK,),
            in_specs=[
                pl.BlockSpec((1, senders, rows3, width), lambda i, info: (info[0], 0, 0, 0), pipeline_mode=once),
                pl.BlockSpec((1, 2, window, width), lambda i, info: (0, 0, 0, 0), pipeline_mode=once),
                pl.BlockSpec((1, 2, SINK_PAD, width), lambda i, info: (0, 0, 0, 0), pipeline_mode=once),
                pl.BlockSpec((seq_len, width), lambda i, info: (0, 0), pipeline_mode=once),
                pl.BlockSpec((seq_len, width), lambda i, info: (0, 0), pipeline_mode=once),
            ],
            out_specs=[
                pl.BlockSpec((BLOCK, width), lambda i, info: (i, 0)),
                pl.BlockSpec((1, 2, window, width), lambda i, info: (0, 0, 0, 0), pipeline_mode=once),
            ],
            scratch_shapes=[
                pltpu.VMEM((seq_len, width), jnp.bfloat16),
                pltpu.VMEM((seq_len, width), jnp.bfloat16),
                pltpu.VMEM((block_count, BLOCK, BLOCK), jnp.float32),
                pltpu.VMEM((seq_len + GRAIN, width), jnp.float32),
                pltpu.VMEM((BLOCK, 128), jnp.float32),
                pltpu.VMEM((BLOCK, 128), jnp.float32),
                pltpu.VMEM((BLOCK, width), jnp.float32),
            ],
        ),
        out_shape=[
            jax.ShapeDtypeStruct((seq_len, width), jnp.bfloat16),
            jax.ShapeDtypeStruct(cache.shape, jnp.bfloat16),
        ],
        compiler_params=pltpu.CompilerParams(
            dimension_semantics=("arbitrary",), vmem_limit_bytes=48 << 20
        ),
        interpret=interpret,
        name="attend",
    )(info, arrived, cache, sink, cosine, sine)


def on_device(
    hidden,
    q_new,
    k_new,
    v_new,
    routes,
    slot_request,
    lengths,
    cycle_cache,
    sink_cache,
    w_out,
    norm_gain,
    router,
    w_gate,
    w_up,
    w_down,
):
    group_width = lax.axis_size("exp")
    group_count = lax.axis_size("req")
    devices_all = group_count * group_width
    group_index = lax.axis_index("req")
    member_index = lax.axis_index("exp")
    slots_here, local_rows, model_width = hidden.shape
    head_count = q_new.shape[1]
    head_dim = q_new.shape[3]
    experts_all = router.shape[1]
    slots_all = slot_request.shape[0]
    seq_len = local_rows * group_width
    tokens = slots_here * local_rows

    held = jnp.clip(slot_request - group_index * slots_here, 0, slots_here - 1)
    source_group = slot_request // slots_here

    def laid_out(part):
        chosen = part[0][None]
        for index in range(1, slots_here):
            flag = (held == index).reshape((slots_all,) + (1,) * (part.ndim - 1))
            chosen = jnp.where(flag, part[index][None], chosen)
        return chosen

    outgoing = laid_out(jnp.concatenate([q_new, k_new, v_new], axis=2))
    outgoing = outgoing.reshape(devices_all, 3 * local_rows, head_dim)
    arrived = lax.all_to_all(outgoing, ("req", "exp"), split_axis=0, concat_axis=0, tiled=True)
    arrived = arrived.reshape(group_count, group_width, 3 * local_rows, head_dim)

    routes_wide = jnp.pad(
        routes.astype(jnp.bfloat16), ((0, 0), (0, 0), (0, 128 - routes.shape[2]))
    )
    states = laid_out(jnp.concatenate([hidden, routes_wide], axis=2))
    states = states.reshape(group_count, tokens, model_width + 128)
    states, arrived = lax.optimization_barrier((states, arrived))
    states = lax.all_to_all(states, "req", split_axis=0, concat_axis=0, tiled=True)

    def picked_states(states):
        states = states.reshape(group_count, slots_here, local_rows, model_width + 128)
        own_sources = lax.dynamic_slice_in_dim(
            source_group, group_index * slots_here, slots_here
        )
        states = jnp.concatenate(
            [
                lax.dynamic_index_in_dim(states[:, slot], own_sources[slot], 0, keepdims=False)
                for slot in range(slots_here)
            ],
            0,
        )
        hidden_sel = states[:, :model_width]
        route_sel = states[:, model_width : model_width + routes.shape[2]].astype(jnp.int32)
        return hidden_sel, route_sel

    slot_here = group_index * slots_here + member_index // head_count
    length = lax.dynamic_index_in_dim(lengths, slot_here, 0, keepdims=False)
    source = lax.dynamic_index_in_dim(source_group, slot_here, 0, keepdims=False)
    cosine, sine = rotary_tables(length, seq_len, head_dim)
    sink_count = sink_cache.shape[2]
    sink_padded = jnp.pad(sink_cache, ((0, 0), (0, 0), (0, SINK_PAD - sink_count), (0, 0)))
    info = jnp.stack([source, length, jnp.int32(sink_count)]).astype(jnp.int32)
    context, cycle_out = attend(info, arrived, cycle_cache, sink_padded, cosine, sine)

    context, states = lax.optimization_barrier((context, states))
    hidden_sel, route_sel = picked_states(states)
    context_rows = lax.all_to_all(
        context.reshape(group_width, local_rows, head_dim),
        "exp",
        split_axis=0,
        concat_axis=0,
        tiled=True,
    ).reshape(slots_here, head_count, local_rows, head_dim)
    context_rows = jnp.transpose(context_rows, (0, 2, 1, 3)).reshape(tokens, head_count * head_dim)
    projected = jnp.dot(context_rows, w_out, preferred_element_type=jnp.float32)
    residual = hidden_sel.astype(jnp.float32) + projected
    inverse = lax.rsqrt(jnp.mean(residual * residual, axis=-1, keepdims=True) + 1e-06)
    normed = (residual * inverse * norm_gain).astype(jnp.bfloat16)

    logits = lax.dot_general(
        router, normed, (((0,), (1,)), ((), ())), preferred_element_type=jnp.float32
    )
    expert_ids = jnp.arange(experts_all, dtype=jnp.int32)
    named = jnp.any(route_sel.T[None] == expert_ids[:, None, None], axis=1)
    token_ids = jnp.arange(tokens, dtype=jnp.int32)
    token_slot = token_ids // local_rows
    before = (token_ids[:, None] < token_ids[None, :]) & (
        token_slot[:, None] == token_slot[None, :]
    )
    ranks = jnp.dot(
        named.astype(jnp.bfloat16), before.astype(jnp.bfloat16), preferred_element_type=jnp.float32
    ).astype(jnp.int32)
    masked = jnp.where(named, logits, -jnp.inf)
    raised = jnp.exp(masked - jnp.max(masked, axis=0, keepdims=True))
    gates = raised / jnp.sum(raised, axis=0, keepdims=True)
    seats = jnp.arange(MOST, dtype=jnp.int32)[None, :, None]
    seated = named[:, None, :] & (ranks[:, None, :] == seats)
    shares = jnp.where(seated, gates[:, None, :], 0.0)

    core_groups = [list(range(core, devices_all, SPLIT)) for core in range(SPLIT)]
    swap = [(index, index ^ 1) for index in range(group_width)]

    def exchanged(rows):
        return lax.all_to_all(
            rows.reshape(experts_all, MOST, model_width),
            ("req", "exp"),
            split_axis=0,
            concat_axis=0,
            axis_index_groups=core_groups,
            tiled=True,
        ).reshape(experts_all * MOST, model_width)

    def piece(rows):
        gate_part = jnp.dot(rows, w_gate, preferred_element_type=jnp.float32)
        up_part = jnp.dot(rows, w_up, preferred_element_type=jnp.float32)
        active = (jax.nn.silu(gate_part) * up_part).astype(jnp.bfloat16)
        return jnp.dot(active, w_down, preferred_element_type=jnp.float32).astype(jnp.bfloat16)

    def expert_rows(rows):
        other_rows = lax.ppermute(rows, "exp", swap)
        own_piece = piece(rows)
        other_piece = lax.ppermute(piece(other_rows), "exp", swap)
        return (own_piece.astype(jnp.float32) + other_piece.astype(jnp.float32)).astype(
            jnp.bfloat16
        )

    def slot_part(array, slot):
        return array[..., slot * local_rows : (slot + 1) * local_rows].reshape(
            experts_all * MOST, local_rows
        )

    def dispatched(slot):
        return jnp.dot(
            slot_part(seated, slot).astype(jnp.bfloat16),
            normed[slot * local_rows : (slot + 1) * local_rows],
            preferred_element_type=jnp.float32,
        ).astype(jnp.bfloat16)

    def combined(slot, returned):
        part = slot_part(shares, slot)
        coarse = lax.reduce_precision(part, 8, 7)
        fine = (part - coarse).astype(jnp.bfloat16)
        both = jnp.concatenate([coarse.astype(jnp.bfloat16), fine], axis=1)
        moe = lax.dot_general(
            both, returned, (((0,), (0,)), ((), ())), preferred_element_type=jnp.float32
        )
        kept = residual[slot * local_rows : (slot + 1) * local_rows]
        return (kept + (moe[:local_rows] + moe[local_rows:])).astype(jnp.bfloat16)

    sent = [dispatched(slot) for slot in range(slots_here)]
    received = []
    for slot in range(slots_here):
        if slot:
            sent[slot], received[slot - 1] = lax.optimization_barrier(
                (sent[slot], received[slot - 1])
            )
        received.append(exchanged(sent[slot]))
    outputs = []
    for slot in range(slots_here):
        answer = expert_rows(received[slot])
        if slot + 1 < slots_here:
            answer, received[slots_here - 1] = lax.optimization_barrier(
                (answer, received[slots_here - 1])
            )
        outputs.append(exchanged(answer))
    layer_out = jnp.stack([combined(slot, outputs[slot]) for slot in range(slots_here)])
    return (layer_out, cycle_out)


def solution(mesh):
    in_specs = (
        P("req", "exp", None),
        P("req", None, "exp", None),
        P("req", None, "exp", None),
        P("req", None, "exp", None),
        P("req", "exp", None),
        P(),
        P(),
        P(("req", "exp"), None, None, None),
        P(("req", "exp"), None, None, None),
        P(),
        P(),
        P(),
        P(None, ("req", "exp")),
        P(None, ("req", "exp")),
        P(("req", "exp"), None),
    )
    out_specs = (P("req", "exp", None), P(("req", "exp"), None, None, None))

    return jax.shard_map(
        on_device, mesh=mesh, in_specs=in_specs, out_specs=out_specs, check_vma=False
    )
```

```python
import math

import jax
import jax.numpy as jnp
from jax import lax
from jax.experimental import pallas as pl
from jax.experimental.pallas import tpu as pltpu
from jax.sharding import PartitionSpec as P


SPLIT = 2
MOST = 8
BLOCK = 512
SINK_PAD = 128
GRAIN = 16
EXPERT_ROWS = 512
CHUNKS = 1


def rotary_tables(length, count, width):
    half_width = width // 2
    frequency = 10000.0 ** (-2.0 * jnp.arange(half_width, dtype=jnp.float32) / width)
    positions = length + jnp.arange(count, dtype=jnp.int32)
    angles = positions.astype(jnp.float32)[:, None] * frequency[None, :]
    cosine = jnp.cos(angles)
    sine = jnp.sin(angles)
    return (
        jnp.concatenate([cosine, cosine], axis=1),
        jnp.concatenate([-sine, sine], axis=1),
    )


def attention_kernel(
    info, arrived, cache, sink, cosine, sine, context, cache_out, k_rot, v_new, scores, shifted, top_acc, sum_acc, out_acc
):
    step = pl.program_id(0)
    length = info[0]
    window = cache.shape[2]
    rows = arrived.shape[2] // 3
    parts = arrived.shape[0]
    seq_len = parts * arrived.shape[1] * rows
    width = arrived.shape[3]
    chunks = BLOCK // (rows * parts)
    turn = lax.rem(length, window)

    def gathered(first_chunk, kind):
        return jnp.concatenate(
            [
                arrived[part, first_chunk + chunk, kind * rows : (kind + 1) * rows, :]
                for chunk in range(chunks)
                for part in range(parts)
            ],
            0,
        )

    def rotated(first_chunk, row_from, kind):
        raw = gathered(first_chunk, kind).astype(jnp.float32)
        cos_rows = cosine[pl.ds(row_from, BLOCK), :]
        sin_rows = sine[pl.ds(row_from, BLOCK), :]
        return raw * cos_rows + pltpu.roll(raw, width // 2, 1) * sin_rows

    @pl.when(step == 0)
    def _():
        for part in range(seq_len // BLOCK):
            k_rot[part * BLOCK : (part + 1) * BLOCK, :] = rotated(
                part * chunks, part * BLOCK, 1
            ).astype(jnp.bfloat16)
            v_new[part * BLOCK : (part + 1) * BLOCK, :] = gathered(part * chunks, 2)
        shift = lax.rem(turn, GRAIN)
        base = turn - shift
        last = lax.rem(base + seq_len, window)
        for kind, fresh in ((0, k_rot), (1, v_new)):
            cache_out[0, kind] = cache[0, kind]
            shifted[0:GRAIN, :] = cache[
                0, kind, pl.ds(pl.multiple_of(base, GRAIN), GRAIN), :
            ].astype(jnp.float32)
            shifted[seq_len : seq_len + GRAIN, :] = cache[
                0, kind, pl.ds(pl.multiple_of(last, GRAIN), GRAIN), :
            ].astype(jnp.float32)
            shifted[pl.ds(shift, seq_len), :] = fresh[...].astype(jnp.float32)

            def place(index, carry):
                target = pl.multiple_of(lax.rem(base + index * GRAIN, window), GRAIN)
                cache_out[0, kind, pl.ds(target, GRAIN), :] = shifted[
                    pl.ds(pl.multiple_of(index * GRAIN, GRAIN), GRAIN), :
                ].astype(jnp.bfloat16)
                return carry

            lax.fori_loop(0, seq_len // GRAIN + 1, place, 0)

    first_row = step * BLOCK
    query = rotated(step * chunks, first_row, 0).astype(jnp.bfloat16)
    row_ids = first_row + lax.broadcasted_iota(jnp.int32, (BLOCK, 1), 0)
    cycle_blocks = window // BLOCK
    new_blocks = seq_len // BLOCK
    sink_block = cycle_blocks + new_blocks
    contract_last = (((1,), (1,)), ((), ()))

    def score(keys):
        return lax.dot_general(query, keys, contract_last, preferred_element_type=jnp.float32)

    def note(block, values):
        best = top_acc[...]
        for lane in range(values.shape[1] // 128):
            best = jnp.maximum(best, values[:, lane * 128 : (lane + 1) * 128])
        top_acc[...] = best
        if values.shape[1] == BLOCK:
            scores[block] = values
        else:
            scores[block, :, 0 : values.shape[1]] = values

    lowest = jnp.float32(-jnp.inf)
    top_acc[...] = jnp.full_like(top_acc, -jnp.inf)

    def order_from(block):
        return lax.rem(block * BLOCK - turn + window, window)

    def cycle_seen(block):
        end = order_from(block) + BLOCK - 1
        return (end > first_row) & (end >= window - length)

    def score_cycle(block, carry):
        start = order_from(block)
        whole = (
            (start + BLOCK <= window)
            & (start > first_row + BLOCK - 1)
            & (start >= window - length)
        )
        keys_at = pl.ds(pl.multiple_of(block * BLOCK, BLOCK), BLOCK)

        @pl.when(whole)
        def _():
            note(block, score(cache[0, 0, keys_at, :]))

        @pl.when(cycle_seen(block) & jnp.logical_not(whole))
        def _():
            order = lax.rem(start + lax.broadcasted_iota(jnp.int32, (1, BLOCK), 1), window)
            order = jnp.where(order >= window - length, order, -1)
            note(block, jnp.where(order > row_ids, score(cache[0, 0, keys_at, :]), lowest))

        return carry

    lax.fori_loop(0, cycle_blocks, score_cycle, 0)

    def score_new(block, carry):
        keys_at = pl.ds(pl.multiple_of(block * BLOCK, BLOCK), BLOCK)
        note(cycle_blocks + block, score(k_rot[keys_at, :]))
        return carry

    lax.fori_loop(0, step, score_new, 0)
    own_at = pl.ds(pl.multiple_of(first_row, BLOCK), BLOCK)
    columns = first_row + lax.broadcasted_iota(jnp.int32, (1, BLOCK), 1)
    note(cycle_blocks + step, jnp.where(columns <= row_ids, score(k_rot[own_at, :]), lowest))
    sink_columns = lax.broadcasted_iota(jnp.int32, (1, SINK_PAD), 1)
    sink_columns = jnp.where(sink_columns < info[1], sink_columns, window + 2 * seq_len + length)
    note(
        sink_block,
        jnp.where(sink_columns <= length + row_ids - window, score(sink[0, 0]), lowest),
    )

    top = jnp.max(top_acc[...], axis=1, keepdims=True)
    factor = jnp.float32(width ** (-0.5) * math.log2(math.e))

    def weights_of(values):
        return jnp.exp2((values - top) * factor)

    def add_up(weights, values):
        total = sum_acc[...]
        for lane in range(weights.shape[1] // 128):
            total = total + weights[:, lane * 128 : (lane + 1) * 128]
        sum_acc[...] = total
        out_acc[...] += jnp.dot(
            weights.astype(jnp.bfloat16), values, preferred_element_type=jnp.float32
        )

    sink_weights = weights_of(scores[sink_block, :, 0:SINK_PAD])
    sum_acc[...] = sink_weights
    out_acc[...] = jnp.dot(
        sink_weights.astype(jnp.bfloat16), sink[0, 1], preferred_element_type=jnp.float32
    )

    def blend_cycle(block, carry):
        @pl.when(cycle_seen(block))
        def _():
            add_up(
                weights_of(scores[block]),
                cache[0, 1, pl.ds(pl.multiple_of(block * BLOCK, BLOCK), BLOCK), :],
            )

        return carry

    lax.fori_loop(0, cycle_blocks, blend_cycle, 0)

    def blend_new(block, carry):
        add_up(
            weights_of(scores[cycle_blocks + block]),
            v_new[pl.ds(pl.multiple_of(block * BLOCK, BLOCK), BLOCK), :],
        )
        return carry

    lax.fori_loop(0, step + 1, blend_new, 0)
    total = jnp.sum(sum_acc[...], axis=1, keepdims=True)
    context[...] = (out_acc[...] / total).astype(jnp.bfloat16)


def attend(info, arrived, cache, sink, cosine, sine, interpret=False):
    groups, senders, rows3, width = arrived.shape
    seq_len = groups * senders * (rows3 // 3)
    window = cache.shape[2]
    block_count = window // BLOCK + seq_len // BLOCK + 1
    once = pl.Buffered(1)
    return pl.pallas_call(
        attention_kernel,
        grid_spec=pltpu.PrefetchScalarGridSpec(
            num_scalar_prefetch=1,
            grid=(seq_len // BLOCK,),
            in_specs=[
                pl.BlockSpec((groups, senders, rows3, width), lambda i, info: (0, 0, 0, 0), pipeline_mode=once),
                pl.BlockSpec((1, 2, window, width), lambda i, info: (0, 0, 0, 0), pipeline_mode=once),
                pl.BlockSpec((1, 2, SINK_PAD, width), lambda i, info: (0, 0, 0, 0), pipeline_mode=once),
                pl.BlockSpec((seq_len, width), lambda i, info: (0, 0), pipeline_mode=once),
                pl.BlockSpec((seq_len, width), lambda i, info: (0, 0), pipeline_mode=once),
            ],
            out_specs=[
                pl.BlockSpec((BLOCK, width), lambda i, info: (i, 0)),
                pl.BlockSpec((1, 2, window, width), lambda i, info: (0, 0, 0, 0), pipeline_mode=once),
            ],
            scratch_shapes=[
                pltpu.VMEM((seq_len, width), jnp.bfloat16),
                pltpu.VMEM((seq_len, width), jnp.bfloat16),
                pltpu.VMEM((block_count, BLOCK, BLOCK), jnp.float32),
                pltpu.VMEM((seq_len + GRAIN, width), jnp.float32),
                pltpu.VMEM((BLOCK, 128), jnp.float32),
                pltpu.VMEM((BLOCK, 128), jnp.float32),
                pltpu.VMEM((BLOCK, width), jnp.float32),
            ],
        ),
        out_shape=[
            jax.ShapeDtypeStruct((seq_len, width), jnp.bfloat16),
            jax.ShapeDtypeStruct(cache.shape, jnp.bfloat16),
        ],
        compiler_params=pltpu.CompilerParams(
            dimension_semantics=("arbitrary",), vmem_limit_bytes=48 << 20
        ),
        interpret=interpret,
        name="attend",
    )(info, arrived, cache, sink, cosine, sine)


def pick_kernel(order, source, target):
    target[...] = source[...]


def pick_rows(order, source):
    block = (1,) + source.shape[1:]
    zeros = (0,) * (source.ndim - 1)
    return pl.pallas_call(
        pick_kernel,
        grid_spec=pltpu.PrefetchScalarGridSpec(
            num_scalar_prefetch=1,
            grid=(order.shape[0],),
            in_specs=[pl.BlockSpec(block, lambda i, order: (order[i],) + zeros)],
            out_specs=pl.BlockSpec(block, lambda i, order: (i,) + zeros),
        ),
        out_shape=jax.ShapeDtypeStruct((order.shape[0],) + source.shape[1:], source.dtype),
        compiler_params=pltpu.CompilerParams(dimension_semantics=("arbitrary",)),
        name="pick_rows",
    )(order, source)


def expert_kernel(
    rows, gate_a, up_a, down_a, gate_b, up_b, down_b, answer, gate_v, up_v, down_v, first, sems
):
    piece = pl.program_id(0)
    block = pl.program_id(1)
    size = rows.shape[0]
    sources = ((gate_a, up_a, down_a), (gate_b, up_b, down_b))

    def copies(number):
        targets = (gate_v.at[number], up_v.at[number], down_v.at[number])
        return [
            pltpu.make_async_copy(source, target, sems.at[number, index])
            for index, (source, target) in enumerate(zip(sources[number], targets))
        ]

    @pl.when((piece == 0) & (block == 0))
    def _():
        for number in range(SPLIT):
            for copy in copies(number):
                copy.start()

    for number in range(SPLIT):

        @pl.when((piece == number) & (block == 0))
        def _():
            for copy in copies(number):
                copy.wait()

    value = rows[...]
    contract_last = (((1,), (1,)), ((), ()))
    gate_part = lax.dot_general(
        value, gate_v[piece], contract_last, preferred_element_type=jnp.float32
    )
    up_part = lax.dot_general(value, up_v[piece], contract_last, preferred_element_type=jnp.float32)
    active = (jax.nn.silu(gate_part) * up_part).astype(jnp.bfloat16)
    output = jnp.dot(active, down_v[piece], preferred_element_type=jnp.float32).astype(jnp.bfloat16)
    at = pl.ds(pl.multiple_of(block * size, size), size)

    @pl.when(piece == 0)
    def _():
        first[at, :] = output

    @pl.when(piece == 1)
    def _():
        answer[...] = (first[at, :].astype(jnp.float32) + output.astype(jnp.float32)).astype(
            jnp.bfloat16
        )


def run_experts(rows, own, other, interpret=False):
    count, model_width = rows.shape
    units = own[0].shape[0]
    size = min(EXPERT_ROWS, count)
    anywhere = pl.BlockSpec(memory_space=pl.ANY)
    return pl.pallas_call(
        expert_kernel,
        grid=(SPLIT, count // size),
        in_specs=[pl.BlockSpec((size, model_width), lambda p, i: (i, 0))] + [anywhere] * 6,
        out_specs=pl.BlockSpec((size, model_width), lambda p, i: (p * i, 0)),
        out_shape=jax.ShapeDtypeStruct(rows.shape, jnp.bfloat16),
        scratch_shapes=[
            pltpu.VMEM((SPLIT, units, model_width), jnp.bfloat16),
            pltpu.VMEM((SPLIT, units, model_width), jnp.bfloat16),
            pltpu.VMEM((SPLIT, units, model_width), jnp.bfloat16),
            pltpu.VMEM(rows.shape, jnp.bfloat16),
            pltpu.SemaphoreType.DMA((SPLIT, 3)),
        ],
        compiler_params=pltpu.CompilerParams(
            dimension_semantics=("arbitrary", "arbitrary"), vmem_limit_bytes=56 << 20
        ),
        interpret=interpret,
        name="run_experts",
    )(rows, *own, *other)


def on_device(
    hidden,
    q_new,
    k_new,
    v_new,
    routes,
    slot_request,
    lengths,
    cycle_cache,
    sink_cache,
    w_out,
    norm_gain,
    router,
    w_gate,
    w_up,
    w_down,
):
    group_width = lax.axis_size("exp")
    group_count = lax.axis_size("req")
    devices_all = group_count * group_width
    group_index = lax.axis_index("req")
    member_index = lax.axis_index("exp")
    slots_here, local_rows, model_width = hidden.shape
    head_count = q_new.shape[1]
    head_dim = q_new.shape[3]
    experts_all = router.shape[1]
    slots_all = slot_request.shape[0]
    seq_len = local_rows * group_width
    tokens = slots_here * local_rows

    held = jnp.clip(slot_request - group_index * slots_here, 0, slots_here - 1)
    source_group = slot_request // slots_here

    def laid_out(part):
        chosen = part[0][None]
        for index in range(1, slots_here):
            flag = (held == index).reshape((slots_all,) + (1,) * (part.ndim - 1))
            chosen = jnp.where(flag, part[index][None], chosen)
        return chosen

    share = local_rows // group_count
    quarters = [
        part.reshape(slots_here, head_count, group_count, share, head_dim)
        for part in (q_new, k_new, v_new)
    ]
    outgoing = jnp.transpose(jnp.concatenate(quarters, axis=3), (2, 0, 1, 3, 4))
    spread = lax.all_to_all(outgoing, "req", split_axis=0, concat_axis=0, tiled=True)
    spread = spread.reshape(slots_all, head_count, 3 * share, head_dim)
    spread = pick_rows(slot_request, spread).reshape(devices_all, 3 * share, head_dim)
    arrived = lax.all_to_all(spread, ("req", "exp"), split_axis=0, concat_axis=0, tiled=True)
    arrived = arrived.reshape(group_count, group_width, 3 * share, head_dim)

    swap = [(index, index ^ 1) for index in range(group_width)]
    own_weights = (w_gate.T, w_up.T, w_down)
    other_weights = tuple(lax.ppermute(part, "exp", swap) for part in own_weights)

    slot_here = group_index * slots_here + member_index // head_count
    length = lax.dynamic_index_in_dim(lengths, slot_here, 0, keepdims=False)
    cosine, sine = rotary_tables(length, seq_len, head_dim)
    sink_count = sink_cache.shape[2]
    sink_padded = jnp.pad(sink_cache, ((0, 0), (0, 0), (0, SINK_PAD - sink_count), (0, 0)))
    info = jnp.stack([length, jnp.int32(sink_count)]).astype(jnp.int32)

    routes_wide = jnp.pad(
        routes.astype(jnp.bfloat16), ((0, 0), (0, 0), (0, 128 - routes.shape[2]))
    )
    states = laid_out(jnp.concatenate([hidden, routes_wide], axis=2))
    states = states.reshape(group_count, tokens, model_width + 128)
    states, arrived, cosine, sine, sink_padded, info, other_weights = lax.optimization_barrier(
        (states, arrived, cosine, sine, sink_padded, info, other_weights)
    )
    states = lax.all_to_all(states, "req", split_axis=0, concat_axis=0, tiled=True)

    def picked_states(states):
        states = states.reshape(group_count, slots_here, local_rows, model_width + 128)
        own_sources = lax.dynamic_slice_in_dim(
            source_group, group_index * slots_here, slots_here
        )
        states = jnp.concatenate(
            [
                lax.dynamic_index_in_dim(states[:, slot], own_sources[slot], 0, keepdims=False)
                for slot in range(slots_here)
            ],
            0,
        )
        hidden_sel = states[:, :model_width]
        route_sel = states[:, model_width : model_width + routes.shape[2]].astype(jnp.int32)
        return hidden_sel, route_sel

    context, cycle_out = attend(info, arrived, cycle_cache, sink_padded, cosine, sine)

    context, states = lax.optimization_barrier((context, states))
    hidden_sel, route_sel = picked_states(states)
    context_rows = lax.all_to_all(
        context.reshape(group_width, local_rows, head_dim),
        "exp",
        split_axis=0,
        concat_axis=0,
        tiled=True,
    ).reshape(slots_here, head_count, local_rows, head_dim)
    context_rows = jnp.transpose(context_rows, (0, 2, 1, 3)).reshape(tokens, head_count * head_dim)
    projected = jnp.dot(context_rows, w_out, preferred_element_type=jnp.float32)
    residual = hidden_sel.astype(jnp.float32) + projected
    inverse = lax.rsqrt(jnp.mean(residual * residual, axis=-1, keepdims=True) + 1e-06)
    normed = (residual * inverse * norm_gain).astype(jnp.bfloat16)

    logits = lax.dot_general(
        router, normed, (((0,), (1,)), ((), ())), preferred_element_type=jnp.float32
    )
    expert_ids = jnp.arange(experts_all, dtype=jnp.int32)
    named = jnp.any(route_sel.T[None] == expert_ids[:, None, None], axis=1)
    token_ids = jnp.arange(tokens, dtype=jnp.int32)
    token_slot = token_ids // local_rows
    before = (token_ids[:, None] < token_ids[None, :]) & (
        token_slot[:, None] == token_slot[None, :]
    )
    ranks = jnp.dot(
        named.astype(jnp.bfloat16), before.astype(jnp.bfloat16), preferred_element_type=jnp.float32
    ).astype(jnp.int32)
    masked = jnp.where(named, logits, -jnp.inf)
    raised = jnp.exp(masked - jnp.max(masked, axis=0, keepdims=True))
    gates = raised / jnp.sum(raised, axis=0, keepdims=True)
    per_chunk = slots_here // CHUNKS
    span = per_chunk * local_rows
    seats = jnp.arange(per_chunk * MOST, dtype=jnp.int32)
    wanted = (token_slot % per_chunk)[None, :] * MOST + ranks
    seated = named[:, None, :] & (wanted[:, None, :] == seats[None, :, None])
    shares = jnp.where(seated, gates[:, None, :], 0.0)
    seats_all = experts_all * per_chunk * MOST

    core_groups = [list(range(core, devices_all, SPLIT)) for core in range(SPLIT)]

    def exchanged(rows):
        return lax.all_to_all(
            rows.reshape(experts_all, per_chunk * MOST, model_width),
            ("req", "exp"),
            split_axis=0,
            concat_axis=0,
            axis_index_groups=core_groups,
            tiled=True,
        ).reshape(seats_all, model_width)

    def slot_part(array, slot):
        return array[..., slot * span : (slot + 1) * span].reshape(seats_all, span)

    def dispatched(slot):
        return jnp.dot(
            slot_part(seated, slot).astype(jnp.bfloat16),
            normed[slot * span : (slot + 1) * span],
            preferred_element_type=jnp.float32,
        ).astype(jnp.bfloat16)

    def combined(slot, returned):
        part = slot_part(shares, slot)
        coarse = lax.reduce_precision(part, 8, 7)
        fine = (part - coarse).astype(jnp.bfloat16)
        both = jnp.concatenate([coarse.astype(jnp.bfloat16), fine], axis=1)
        moe = lax.dot_general(
            both, returned, (((0,), (0,)), ((), ())), preferred_element_type=jnp.float32
        )
        kept = residual[slot * span : (slot + 1) * span]
        return (kept + (moe[:span] + moe[span:])).astype(jnp.bfloat16)

    sent = [dispatched(slot) for slot in range(CHUNKS)]
    received = []
    for slot in range(CHUNKS):
        if slot:
            sent[slot], received[slot - 1] = lax.optimization_barrier(
                (sent[slot], received[slot - 1])
            )
        received.append(exchanged(sent[slot]))
    outputs = []
    for slot in range(CHUNKS):
        answer = run_experts(received[slot], own_weights, other_weights)
        if slot + 1 < CHUNKS:
            answer, received[CHUNKS - 1] = lax.optimization_barrier((answer, received[CHUNKS - 1]))
        outputs.append(exchanged(answer))
    layer_out = jnp.concatenate([combined(slot, outputs[slot]) for slot in range(CHUNKS)])
    layer_out = layer_out.reshape(slots_here, local_rows, model_width)
    return (layer_out, cycle_out)


def solution(mesh):
    in_specs = (
        P("req", "exp", None),
        P("req", None, "exp", None),
        P("req", None, "exp", None),
        P("req", None, "exp", None),
        P("req", "exp", None),
        P(),
        P(),
        P(("req", "exp"), None, None, None),
        P(("req", "exp"), None, None, None),
        P(),
        P(),
        P(),
        P(None, ("req", "exp")),
        P(None, ("req", "exp")),
        P(("req", "exp"), None),
    )
    out_specs = (P("req", "exp", None), P(("req", "exp"), None, None, None))

    return jax.shard_map(
        on_device, mesh=mesh, in_specs=in_specs, out_specs=out_specs, check_vma=False
    )
```

```python
import math

import jax
import jax.numpy as jnp
from jax import lax
from jax.experimental import pallas as pl
from jax.experimental.pallas import tpu as pltpu
from jax.sharding import PartitionSpec as P


SPLIT = 2
MOST = 8
BLOCK = 512
SINK_PAD = 128
GRAIN = 16
EXPERT_ROWS = 512
CHUNKS = 1


def rotary_tables(length, count, width):
    half_width = width // 2
    frequency = 10000.0 ** (-2.0 * jnp.arange(half_width, dtype=jnp.float32) / width)
    positions = length + jnp.arange(count, dtype=jnp.int32)
    angles = positions.astype(jnp.float32)[:, None] * frequency[None, :]
    cosine = jnp.cos(angles)
    sine = jnp.sin(angles)
    return (
        jnp.concatenate([cosine, cosine], axis=1),
        jnp.concatenate([-sine, sine], axis=1),
    )


def attention_kernel(
    info, arrived, cache, sink, cosine, sine, context, cache_out, k_rot, v_new, scores, shifted, top_acc, sum_acc, out_acc
):
    step = pl.program_id(0)
    length = info[0]
    window = cache.shape[2]
    rows = arrived.shape[2] // 3
    parts = arrived.shape[0]
    seq_len = parts * arrived.shape[1] * rows
    width = arrived.shape[3]
    chunks = BLOCK // (rows * parts)
    turn = lax.rem(length, window)

    def gathered(first_chunk, kind):
        return jnp.concatenate(
            [
                arrived[part, first_chunk + chunk, kind * rows : (kind + 1) * rows, :]
                for chunk in range(chunks)
                for part in range(parts)
            ],
            0,
        )

    def rotated(first_chunk, row_from, kind):
        raw = gathered(first_chunk, kind).astype(jnp.float32)
        cos_rows = cosine[pl.ds(row_from, BLOCK), :]
        sin_rows = sine[pl.ds(row_from, BLOCK), :]
        return raw * cos_rows + pltpu.roll(raw, width // 2, 1) * sin_rows

    @pl.when(step == 0)
    def _():
        for part in range(seq_len // BLOCK):
            k_rot[part * BLOCK : (part + 1) * BLOCK, :] = rotated(
                part * chunks, part * BLOCK, 1
            ).astype(jnp.bfloat16)
            v_new[part * BLOCK : (part + 1) * BLOCK, :] = gathered(part * chunks, 2)
        shift = lax.rem(turn, GRAIN)
        base = turn - shift
        last = lax.rem(base + seq_len, window)
        for kind, fresh in ((0, k_rot), (1, v_new)):
            cache_out[0, kind] = cache[0, kind]
            shifted[0:GRAIN, :] = cache[
                0, kind, pl.ds(pl.multiple_of(base, GRAIN), GRAIN), :
            ].astype(jnp.float32)
            shifted[seq_len : seq_len + GRAIN, :] = cache[
                0, kind, pl.ds(pl.multiple_of(last, GRAIN), GRAIN), :
            ].astype(jnp.float32)
            shifted[pl.ds(shift, seq_len), :] = fresh[...].astype(jnp.float32)

            def place(index, carry):
                target = pl.multiple_of(lax.rem(base + index * GRAIN, window), GRAIN)
                cache_out[0, kind, pl.ds(target, GRAIN), :] = shifted[
                    pl.ds(pl.multiple_of(index * GRAIN, GRAIN), GRAIN), :
                ].astype(jnp.bfloat16)
                return carry

            lax.fori_loop(0, seq_len // GRAIN + 1, place, 0)

    first_row = step * BLOCK
    query = rotated(step * chunks, first_row, 0).astype(jnp.bfloat16)
    row_ids = first_row + lax.broadcasted_iota(jnp.int32, (BLOCK, 1), 0)
    cycle_blocks = window // BLOCK
    new_blocks = seq_len // BLOCK
    sink_block = cycle_blocks + new_blocks
    contract_last = (((1,), (1,)), ((), ()))

    def score(keys):
        return lax.dot_general(query, keys, contract_last, preferred_element_type=jnp.float32)

    def note(block, values):
        best = top_acc[...]
        for lane in range(values.shape[1] // 128):
            best = jnp.maximum(best, values[:, lane * 128 : (lane + 1) * 128])
        top_acc[...] = best
        if values.shape[1] == BLOCK:
            scores[block] = values
        else:
            scores[block, :, 0 : values.shape[1]] = values

    lowest = jnp.float32(-jnp.inf)
    top_acc[...] = jnp.full_like(top_acc, -jnp.inf)

    def order_from(block):
        return lax.rem(block * BLOCK - turn + window, window)

    def cycle_seen(block):
        end = order_from(block) + BLOCK - 1
        return (end > first_row) & (end >= window - length)

    def score_cycle(block, carry):
        start = order_from(block)
        whole = (
            (start + BLOCK <= window)
            & (start > first_row + BLOCK - 1)
            & (start >= window - length)
        )
        keys_at = pl.ds(pl.multiple_of(block * BLOCK, BLOCK), BLOCK)

        @pl.when(whole)
        def _():
            note(block, score(cache[0, 0, keys_at, :]))

        @pl.when(cycle_seen(block) & jnp.logical_not(whole))
        def _():
            order = lax.rem(start + lax.broadcasted_iota(jnp.int32, (1, BLOCK), 1), window)
            order = jnp.where(order >= window - length, order, -1)
            note(block, jnp.where(order > row_ids, score(cache[0, 0, keys_at, :]), lowest))

        return carry

    lax.fori_loop(0, cycle_blocks, score_cycle, 0)

    def score_new(block, carry):
        keys_at = pl.ds(pl.multiple_of(block * BLOCK, BLOCK), BLOCK)
        note(cycle_blocks + block, score(k_rot[keys_at, :]))
        return carry

    lax.fori_loop(0, step, score_new, 0)
    own_at = pl.ds(pl.multiple_of(first_row, BLOCK), BLOCK)
    columns = first_row + lax.broadcasted_iota(jnp.int32, (1, BLOCK), 1)
    note(cycle_blocks + step, jnp.where(columns <= row_ids, score(k_rot[own_at, :]), lowest))
    sink_columns = lax.broadcasted_iota(jnp.int32, (1, SINK_PAD), 1)
    sink_columns = jnp.where(sink_columns < info[1], sink_columns, window + 2 * seq_len + length)
    note(
        sink_block,
        jnp.where(sink_columns <= length + row_ids - window, score(sink[0, 0]), lowest),
    )

    top = jnp.max(top_acc[...], axis=1, keepdims=True)
    factor = jnp.float32(width ** (-0.5) * math.log2(math.e))

    def weights_of(values):
        return jnp.exp2((values - top) * factor)

    def add_up(weights, values):
        total = sum_acc[...]
        for lane in range(weights.shape[1] // 128):
            total = total + weights[:, lane * 128 : (lane + 1) * 128]
        sum_acc[...] = total
        out_acc[...] += jnp.dot(
            weights.astype(jnp.bfloat16), values, preferred_element_type=jnp.float32
        )

    sink_weights = weights_of(scores[sink_block, :, 0:SINK_PAD])
    sum_acc[...] = sink_weights
    out_acc[...] = jnp.dot(
        sink_weights.astype(jnp.bfloat16), sink[0, 1], preferred_element_type=jnp.float32
    )

    def blend_cycle(block, carry):
        @pl.when(cycle_seen(block))
        def _():
            add_up(
                weights_of(scores[block]),
                cache[0, 1, pl.ds(pl.multiple_of(block * BLOCK, BLOCK), BLOCK), :],
            )

        return carry

    lax.fori_loop(0, cycle_blocks, blend_cycle, 0)

    def blend_new(block, carry):
        add_up(
            weights_of(scores[cycle_blocks + block]),
            v_new[pl.ds(pl.multiple_of(block * BLOCK, BLOCK), BLOCK), :],
        )
        return carry

    lax.fori_loop(0, step + 1, blend_new, 0)
    total = jnp.sum(sum_acc[...], axis=1, keepdims=True)
    context[...] = (out_acc[...] / total).astype(jnp.bfloat16)


def attend(info, arrived, cache, sink, cosine, sine, interpret=False):
    groups, senders, rows3, width = arrived.shape
    seq_len = groups * senders * (rows3 // 3)
    window = cache.shape[2]
    block_count = window // BLOCK + seq_len // BLOCK + 1
    once = pl.Buffered(1)
    return pl.pallas_call(
        attention_kernel,
        grid_spec=pltpu.PrefetchScalarGridSpec(
            num_scalar_prefetch=1,
            grid=(seq_len // BLOCK,),
            in_specs=[
                pl.BlockSpec((groups, senders, rows3, width), lambda i, info: (0, 0, 0, 0), pipeline_mode=once),
                pl.BlockSpec((1, 2, window, width), lambda i, info: (0, 0, 0, 0), pipeline_mode=once),
                pl.BlockSpec((1, 2, SINK_PAD, width), lambda i, info: (0, 0, 0, 0), pipeline_mode=once),
                pl.BlockSpec((seq_len, width), lambda i, info: (0, 0), pipeline_mode=once),
                pl.BlockSpec((seq_len, width), lambda i, info: (0, 0), pipeline_mode=once),
            ],
            out_specs=[
                pl.BlockSpec((BLOCK, width), lambda i, info: (i, 0)),
                pl.BlockSpec((1, 2, window, width), lambda i, info: (0, 0, 0, 0), pipeline_mode=once),
            ],
            scratch_shapes=[
                pltpu.VMEM((seq_len, width), jnp.bfloat16),
                pltpu.VMEM((seq_len, width), jnp.bfloat16),
                pltpu.VMEM((block_count, BLOCK, BLOCK), jnp.float32),
                pltpu.VMEM((seq_len + GRAIN, width), jnp.float32),
                pltpu.VMEM((BLOCK, 128), jnp.float32),
                pltpu.VMEM((BLOCK, 128), jnp.float32),
                pltpu.VMEM((BLOCK, width), jnp.float32),
            ],
        ),
        out_shape=[
            jax.ShapeDtypeStruct((seq_len, width), jnp.bfloat16),
            jax.ShapeDtypeStruct(cache.shape, jnp.bfloat16),
        ],
        compiler_params=pltpu.CompilerParams(
            dimension_semantics=("arbitrary",), vmem_limit_bytes=48 << 20
        ),
        interpret=interpret,
        name="attend",
    )(info, arrived, cache, sink, cosine, sine)


def pick_kernel(order, source, target, sems):
    copies = [
        pltpu.make_async_copy(source.at[order[slot]], target.at[slot], sems.at[slot])
        for slot in range(target.shape[0])
    ]
    for copy in copies:
        copy.start()
    for copy in copies:
        copy.wait()


def pick_rows(order, source):
    return pl.pallas_call(
        pick_kernel,
        grid_spec=pltpu.PrefetchScalarGridSpec(
            num_scalar_prefetch=1,
            grid=(1,),
            in_specs=[pl.BlockSpec(memory_space=pl.ANY)],
            out_specs=pl.BlockSpec(memory_space=pl.ANY),
            scratch_shapes=[pltpu.SemaphoreType.DMA((order.shape[0],))],
        ),
        out_shape=jax.ShapeDtypeStruct((order.shape[0],) + source.shape[1:], source.dtype),
        name="pick_rows",
    )(order, source)


def expert_kernel(
    rows, gate_a, up_a, down_a, gate_b, up_b, down_b, answer, gate_v, up_v, down_v, first, sems
):
    piece = pl.program_id(0)
    block = pl.program_id(1)
    size = rows.shape[0]
    sources = ((gate_a, up_a, down_a), (gate_b, up_b, down_b))

    def copies(number):
        targets = (gate_v.at[number], up_v.at[number], down_v.at[number])
        return [
            pltpu.make_async_copy(source, target, sems.at[number, index])
            for index, (source, target) in enumerate(zip(sources[number], targets))
        ]

    @pl.when((piece == 0) & (block == 0))
    def _():
        for copy in copies(0):
            copy.start()

    def arrive(index):
        for number in range(SPLIT):

            @pl.when((piece == number) & (block == 0))
            def _():
                copies(number)[index].wait()

    value = rows[...]
    contract_last = (((1,), (1,)), ((), ()))
    arrive(0)
    gate_part = lax.dot_general(
        value, gate_v[piece], contract_last, preferred_element_type=jnp.float32
    )
    arrive(1)
    up_part = lax.dot_general(value, up_v[piece], contract_last, preferred_element_type=jnp.float32)
    active = (jax.nn.silu(gate_part) * up_part).astype(jnp.bfloat16)
    arrive(2)

    @pl.when((piece == 0) & (block == 0))
    def _():
        for copy in copies(1):
            copy.start()

    output = jnp.dot(active, down_v[piece], preferred_element_type=jnp.float32).astype(jnp.bfloat16)
    at = pl.ds(pl.multiple_of(block * size, size), size)

    @pl.when(piece == 0)
    def _():
        first[at, :] = output

    @pl.when(piece == 1)
    def _():
        answer[...] = (first[at, :].astype(jnp.float32) + output.astype(jnp.float32)).astype(
            jnp.bfloat16
        )


def run_experts(rows, own, other, interpret=False):
    count, model_width = rows.shape
    units = own[0].shape[0]
    size = min(EXPERT_ROWS, count)
    anywhere = pl.BlockSpec(memory_space=pl.ANY)
    return pl.pallas_call(
        expert_kernel,
        grid=(SPLIT, count // size),
        in_specs=[pl.BlockSpec((size, model_width), lambda p, i: (i, 0))] + [anywhere] * 6,
        out_specs=pl.BlockSpec((size, model_width), lambda p, i: (p * i, 0)),
        out_shape=jax.ShapeDtypeStruct(rows.shape, jnp.bfloat16),
        scratch_shapes=[
            pltpu.VMEM((SPLIT, units, model_width), jnp.bfloat16),
            pltpu.VMEM((SPLIT, units, model_width), jnp.bfloat16),
            pltpu.VMEM((SPLIT, units, model_width), jnp.bfloat16),
            pltpu.VMEM(rows.shape, jnp.bfloat16),
            pltpu.SemaphoreType.DMA((SPLIT, 3)),
        ],
        compiler_params=pltpu.CompilerParams(
            dimension_semantics=("arbitrary", "arbitrary"), vmem_limit_bytes=56 << 20
        ),
        interpret=interpret,
        name="run_experts",
    )(rows, *own, *other)


def on_device(
    hidden,
    q_new,
    k_new,
    v_new,
    routes,
    slot_request,
    lengths,
    cycle_cache,
    sink_cache,
    w_out,
    norm_gain,
    router,
    w_gate,
    w_up,
    w_down,
):
    group_width = lax.axis_size("exp")
    group_count = lax.axis_size("req")
    devices_all = group_count * group_width
    group_index = lax.axis_index("req")
    member_index = lax.axis_index("exp")
    slots_here, local_rows, model_width = hidden.shape
    head_count = q_new.shape[1]
    head_dim = q_new.shape[3]
    experts_all = router.shape[1]
    slots_all = slot_request.shape[0]
    seq_len = local_rows * group_width
    tokens = slots_here * local_rows

    held = jnp.clip(slot_request - group_index * slots_here, 0, slots_here - 1)
    source_group = slot_request // slots_here

    def laid_out(part):
        chosen = part[0][None]
        for index in range(1, slots_here):
            flag = (held == index).reshape((slots_all,) + (1,) * (part.ndim - 1))
            chosen = jnp.where(flag, part[index][None], chosen)
        return chosen

    share = local_rows // group_count
    quarters = [
        part.reshape(slots_here, head_count, group_count, share, head_dim)
        for part in (q_new, k_new, v_new)
    ]
    outgoing = jnp.transpose(jnp.concatenate(quarters, axis=3), (2, 0, 1, 3, 4))
    spread = lax.all_to_all(outgoing, "req", split_axis=0, concat_axis=0, tiled=True)
    spread = spread.reshape(slots_all, head_count, 3 * share, head_dim)
    spread = pick_rows(slot_request, spread).reshape(devices_all, 3 * share, head_dim)
    arrived = lax.all_to_all(spread, ("req", "exp"), split_axis=0, concat_axis=0, tiled=True)
    arrived = arrived.reshape(group_count, group_width, 3 * share, head_dim)

    swap = [(index, index ^ 1) for index in range(group_width)]
    own_weights = (w_gate.T, w_up.T, w_down)
    other_weights = tuple(lax.ppermute(part, "exp", swap) for part in own_weights)

    slot_here = group_index * slots_here + member_index // head_count
    length = lax.dynamic_index_in_dim(lengths, slot_here, 0, keepdims=False)
    cosine, sine = rotary_tables(length, seq_len, head_dim)
    sink_count = sink_cache.shape[2]
    sink_padded = jnp.pad(sink_cache, ((0, 0), (0, 0), (0, SINK_PAD - sink_count), (0, 0)))
    info = jnp.stack([length, jnp.int32(sink_count)]).astype(jnp.int32)

    routes_wide = jnp.pad(
        routes.astype(jnp.bfloat16), ((0, 0), (0, 0), (0, 128 - routes.shape[2]))
    )
    states = laid_out(jnp.concatenate([hidden, routes_wide], axis=2))
    states = states.reshape(group_count, tokens, model_width + 128)
    states, arrived, cosine, sine, sink_padded, info, other_weights = lax.optimization_barrier(
        (states, arrived, cosine, sine, sink_padded, info, other_weights)
    )
    states = lax.all_to_all(states, "req", split_axis=0, concat_axis=0, tiled=True)

    def picked_states(states):
        states = states.reshape(group_count, slots_here, local_rows, model_width + 128)
        own_sources = lax.dynamic_slice_in_dim(
            source_group, group_index * slots_here, slots_here
        )
        states = jnp.concatenate(
            [
                lax.dynamic_index_in_dim(states[:, slot], own_sources[slot], 0, keepdims=False)
                for slot in range(slots_here)
            ],
            0,
        )
        hidden_sel = states[:, :model_width]
        route_sel = states[:, model_width : model_width + routes.shape[2]].astype(jnp.int32)
        return hidden_sel, route_sel

    context, cycle_out = attend(info, arrived, cycle_cache, sink_padded, cosine, sine)

    context, states = lax.optimization_barrier((context, states))
    hidden_sel, route_sel = picked_states(states)
    context_rows = lax.all_to_all(
        context.reshape(group_width, local_rows, head_dim),
        "exp",
        split_axis=0,
        concat_axis=0,
        tiled=True,
    ).reshape(slots_here, head_count, local_rows, head_dim)
    context_rows = jnp.transpose(context_rows, (0, 2, 1, 3)).reshape(tokens, head_count * head_dim)
    projected = jnp.dot(context_rows, w_out, preferred_element_type=jnp.float32)
    residual = hidden_sel.astype(jnp.float32) + projected
    inverse = lax.rsqrt(jnp.mean(residual * residual, axis=-1, keepdims=True) + 1e-06)
    normed = (residual * inverse * norm_gain).astype(jnp.bfloat16)

    logits = lax.dot_general(
        router, normed, (((0,), (1,)), ((), ())), preferred_element_type=jnp.float32
    )
    expert_ids = jnp.arange(experts_all, dtype=jnp.int32)
    named = jnp.any(route_sel.T[None] == expert_ids[:, None, None], axis=1)
    token_ids = jnp.arange(tokens, dtype=jnp.int32)
    token_slot = token_ids // local_rows
    before = (token_ids[:, None] < token_ids[None, :]) & (
        token_slot[:, None] == token_slot[None, :]
    )
    ranks = jnp.dot(
        named.astype(jnp.bfloat16), before.astype(jnp.bfloat16), preferred_element_type=jnp.float32
    ).astype(jnp.int32)
    masked = jnp.where(named, logits, -jnp.inf)
    raised = jnp.exp(masked - jnp.max(masked, axis=0, keepdims=True))
    gates = raised / jnp.sum(raised, axis=0, keepdims=True)
    per_chunk = slots_here // CHUNKS
    span = per_chunk * local_rows
    seats = jnp.arange(per_chunk * MOST, dtype=jnp.int32)
    wanted = (token_slot % per_chunk)[None, :] * MOST + ranks
    seated = named[:, None, :] & (wanted[:, None, :] == seats[None, :, None])
    shares = jnp.where(seated, gates[:, None, :], 0.0)
    seats_all = experts_all * per_chunk * MOST

    def exchanged(rows):
        return lax.all_to_all(
            rows.reshape(devices_all, seats_all // devices_all, model_width),
            ("req", "exp"),
            split_axis=0,
            concat_axis=0,
            tiled=True,
        ).reshape(seats_all, model_width)

    def slot_part(array, slot):
        return array[..., slot * span : (slot + 1) * span].reshape(seats_all, span)

    def dispatched(slot):
        return jnp.dot(
            slot_part(seated, slot).astype(jnp.bfloat16),
            normed[slot * span : (slot + 1) * span],
            preferred_element_type=jnp.float32,
        ).astype(jnp.bfloat16)

    def combined(slot, returned):
        part = slot_part(shares, slot)
        coarse = lax.reduce_precision(part, 8, 7)
        fine = (part - coarse).astype(jnp.bfloat16)
        both = jnp.concatenate([coarse.astype(jnp.bfloat16), fine], axis=1)
        moe = lax.dot_general(
            both, returned, (((0,), (0,)), ((), ())), preferred_element_type=jnp.float32
        )
        kept = residual[slot * span : (slot + 1) * span]
        return (kept + (moe[:span] + moe[span:])).astype(jnp.bfloat16)

    sent = [dispatched(slot) for slot in range(CHUNKS)]
    received = []
    for slot in range(CHUNKS):
        if slot:
            sent[slot], received[slot - 1] = lax.optimization_barrier(
                (sent[slot], received[slot - 1])
            )
        received.append(exchanged(sent[slot]))
    outputs = []
    for slot in range(CHUNKS):
        answer = run_experts(received[slot], own_weights, other_weights)
        if slot + 1 < CHUNKS:
            answer, received[CHUNKS - 1] = lax.optimization_barrier((answer, received[CHUNKS - 1]))
        outputs.append(exchanged(answer))
    layer_out = jnp.concatenate([combined(slot, outputs[slot]) for slot in range(CHUNKS)])
    layer_out = layer_out.reshape(slots_here, local_rows, model_width)
    return (layer_out, cycle_out)


def solution(mesh):
    in_specs = (
        P("req", "exp", None),
        P("req", None, "exp", None),
        P("req", None, "exp", None),
        P("req", None, "exp", None),
        P("req", "exp", None),
        P(),
        P(),
        P(("req", "exp"), None, None, None),
        P(("req", "exp"), None, None, None),
        P(),
        P(),
        P(),
        P(None, ("req", "exp")),
        P(None, ("req", "exp")),
        P(("req", "exp"), None),
    )
    out_specs = (P("req", "exp", None), P(("req", "exp"), None, None, None))

    return jax.shard_map(
        on_device, mesh=mesh, in_specs=in_specs, out_specs=out_specs, check_vma=False
    )
```

```python
import math

import jax
import jax.numpy as jnp
from jax import lax
from jax.experimental import pallas as pl
from jax.experimental.pallas import tpu as pltpu
from jax.sharding import PartitionSpec as P


SPLIT = 2
MOST = 8
BLOCK = 512
SINK_PAD = 128
GRAIN = 16
EXPERT_ROWS = 512
CHUNKS = 1


def rotary_tables(length, count, width):
    half_width = width // 2
    frequency = 10000.0 ** (-2.0 * jnp.arange(half_width, dtype=jnp.float32) / width)
    positions = length + jnp.arange(count, dtype=jnp.int32)
    angles = positions.astype(jnp.float32)[:, None] * frequency[None, :]
    cosine = jnp.cos(angles)
    sine = jnp.sin(angles)
    return (
        jnp.concatenate([cosine, cosine], axis=1),
        jnp.concatenate([-sine, sine], axis=1),
    )


def attention_kernel(
    info, arrived, cache, sink, cosine, sine, context, cache_out, k_rot, v_new, scores, shifted, top_acc, sum_acc, out_acc
):
    step = pl.program_id(0)
    length = info[0]
    window = cache.shape[2]
    rows = arrived.shape[2] // 3
    parts = arrived.shape[0]
    seq_len = parts * arrived.shape[1] * rows
    width = arrived.shape[3]
    chunks = BLOCK // (rows * parts)
    turn = lax.rem(length, window)

    def gathered(first_chunk, kind):
        return jnp.concatenate(
            [
                arrived[part, first_chunk + chunk, kind * rows : (kind + 1) * rows, :]
                for chunk in range(chunks)
                for part in range(parts)
            ],
            0,
        )

    def rotated(first_chunk, row_from, kind):
        raw = gathered(first_chunk, kind).astype(jnp.float32)
        cos_rows = cosine[pl.ds(row_from, BLOCK), :]
        sin_rows = sine[pl.ds(row_from, BLOCK), :]
        return raw * cos_rows + pltpu.roll(raw, width // 2, 1) * sin_rows

    @pl.when(step == 0)
    def _():
        for part in range(seq_len // BLOCK):
            k_rot[part * BLOCK : (part + 1) * BLOCK, :] = rotated(
                part * chunks, part * BLOCK, 1
            ).astype(jnp.bfloat16)
            v_new[part * BLOCK : (part + 1) * BLOCK, :] = gathered(part * chunks, 2)
        shift = lax.rem(turn, GRAIN)
        base = turn - shift
        last = lax.rem(base + seq_len, window)
        for kind, fresh in ((0, k_rot), (1, v_new)):
            cache_out[0, kind] = cache[0, kind]
            shifted[0:GRAIN, :] = cache[
                0, kind, pl.ds(pl.multiple_of(base, GRAIN), GRAIN), :
            ].astype(jnp.float32)
            shifted[seq_len : seq_len + GRAIN, :] = cache[
                0, kind, pl.ds(pl.multiple_of(last, GRAIN), GRAIN), :
            ].astype(jnp.float32)
            shifted[pl.ds(shift, seq_len), :] = fresh[...].astype(jnp.float32)

            def place(index, carry):
                target = pl.multiple_of(lax.rem(base + index * GRAIN, window), GRAIN)
                cache_out[0, kind, pl.ds(target, GRAIN), :] = shifted[
                    pl.ds(pl.multiple_of(index * GRAIN, GRAIN), GRAIN), :
                ].astype(jnp.bfloat16)
                return carry

            lax.fori_loop(0, seq_len // GRAIN + 1, place, 0)

    first_row = step * BLOCK
    query = rotated(step * chunks, first_row, 0).astype(jnp.bfloat16)
    row_ids = first_row + lax.broadcasted_iota(jnp.int32, (BLOCK, 1), 0)
    cycle_blocks = window // BLOCK
    new_blocks = seq_len // BLOCK
    sink_block = cycle_blocks + new_blocks
    contract_last = (((1,), (1,)), ((), ()))

    def score(keys):
        return lax.dot_general(query, keys, contract_last, preferred_element_type=jnp.float32)

    def note(block, values):
        best = top_acc[...]
        for lane in range(values.shape[1] // 128):
            best = jnp.maximum(best, values[:, lane * 128 : (lane + 1) * 128])
        top_acc[...] = best
        if values.shape[1] == BLOCK:
            scores[block] = values
        else:
            scores[block, :, 0 : values.shape[1]] = values

    lowest = jnp.float32(-jnp.inf)
    top_acc[...] = jnp.full_like(top_acc, -jnp.inf)

    def order_from(block):
        return lax.rem(block * BLOCK - turn + window, window)

    def cycle_seen(block):
        end = order_from(block) + BLOCK - 1
        return (end > first_row) & (end >= window - length)

    def score_cycle(block, carry):
        start = order_from(block)
        whole = (
            (start + BLOCK <= window)
            & (start > first_row + BLOCK - 1)
            & (start >= window - length)
        )
        keys_at = pl.ds(pl.multiple_of(block * BLOCK, BLOCK), BLOCK)

        @pl.when(whole)
        def _():
            note(block, score(cache[0, 0, keys_at, :]))

        @pl.when(cycle_seen(block) & jnp.logical_not(whole))
        def _():
            order = lax.rem(start + lax.broadcasted_iota(jnp.int32, (1, BLOCK), 1), window)
            order = jnp.where(order >= window - length, order, -1)
            note(block, jnp.where(order > row_ids, score(cache[0, 0, keys_at, :]), lowest))

        return carry

    lax.fori_loop(0, cycle_blocks, score_cycle, 0)

    def score_new(block, carry):
        keys_at = pl.ds(pl.multiple_of(block * BLOCK, BLOCK), BLOCK)
        note(cycle_blocks + block, score(k_rot[keys_at, :]))
        return carry

    lax.fori_loop(0, step, score_new, 0)
    own_at = pl.ds(pl.multiple_of(first_row, BLOCK), BLOCK)
    columns = first_row + lax.broadcasted_iota(jnp.int32, (1, BLOCK), 1)
    note(cycle_blocks + step, jnp.where(columns <= row_ids, score(k_rot[own_at, :]), lowest))
    sink_columns = lax.broadcasted_iota(jnp.int32, (1, SINK_PAD), 1)
    sink_columns = jnp.where(sink_columns < info[1], sink_columns, window + 2 * seq_len + length)
    note(
        sink_block,
        jnp.where(sink_columns <= length + row_ids - window, score(sink[0, 0]), lowest),
    )

    top = jnp.max(top_acc[...], axis=1, keepdims=True)
    factor = jnp.float32(width ** (-0.5) * math.log2(math.e))

    def weights_of(values):
        return jnp.exp2((values - top) * factor)

    def add_up(weights, values):
        total = sum_acc[...]
        for lane in range(weights.shape[1] // 128):
            total = total + weights[:, lane * 128 : (lane + 1) * 128]
        sum_acc[...] = total
        out_acc[...] += jnp.dot(
            weights.astype(jnp.bfloat16), values, preferred_element_type=jnp.float32
        )

    sink_weights = weights_of(scores[sink_block, :, 0:SINK_PAD])
    sum_acc[...] = sink_weights
    out_acc[...] = jnp.dot(
        sink_weights.astype(jnp.bfloat16), sink[0, 1], preferred_element_type=jnp.float32
    )

    def blend_cycle(block, carry):
        @pl.when(cycle_seen(block))
        def _():
            add_up(
                weights_of(scores[block]),
                cache[0, 1, pl.ds(pl.multiple_of(block * BLOCK, BLOCK), BLOCK), :],
            )

        return carry

    lax.fori_loop(0, cycle_blocks, blend_cycle, 0)

    def blend_new(block, carry):
        add_up(
            weights_of(scores[cycle_blocks + block]),
            v_new[pl.ds(pl.multiple_of(block * BLOCK, BLOCK), BLOCK), :],
        )
        return carry

    lax.fori_loop(0, step + 1, blend_new, 0)
    total = jnp.sum(sum_acc[...], axis=1, keepdims=True)
    context[...] = (out_acc[...] / total).astype(jnp.bfloat16)


def attend(info, arrived, cache, sink, cosine, sine, interpret=False):
    groups, senders, rows3, width = arrived.shape
    seq_len = groups * senders * (rows3 // 3)
    window = cache.shape[2]
    block_count = window // BLOCK + seq_len // BLOCK + 1
    once = pl.Buffered(1)
    return pl.pallas_call(
        attention_kernel,
        grid_spec=pltpu.PrefetchScalarGridSpec(
            num_scalar_prefetch=1,
            grid=(seq_len // BLOCK,),
            in_specs=[
                pl.BlockSpec((groups, senders, rows3, width), lambda i, info: (0, 0, 0, 0), pipeline_mode=once),
                pl.BlockSpec((1, 2, window, width), lambda i, info: (0, 0, 0, 0), pipeline_mode=once),
                pl.BlockSpec((1, 2, SINK_PAD, width), lambda i, info: (0, 0, 0, 0), pipeline_mode=once),
                pl.BlockSpec((seq_len, width), lambda i, info: (0, 0), pipeline_mode=once),
                pl.BlockSpec((seq_len, width), lambda i, info: (0, 0), pipeline_mode=once),
            ],
            out_specs=[
                pl.BlockSpec((BLOCK, width), lambda i, info: (i, 0)),
                pl.BlockSpec((1, 2, window, width), lambda i, info: (0, 0, 0, 0), pipeline_mode=once),
            ],
            scratch_shapes=[
                pltpu.VMEM((seq_len, width), jnp.bfloat16),
                pltpu.VMEM((seq_len, width), jnp.bfloat16),
                pltpu.VMEM((block_count, BLOCK, BLOCK), jnp.float32),
                pltpu.VMEM((seq_len + GRAIN, width), jnp.float32),
                pltpu.VMEM((BLOCK, 128), jnp.float32),
                pltpu.VMEM((BLOCK, 128), jnp.float32),
                pltpu.VMEM((BLOCK, width), jnp.float32),
            ],
        ),
        out_shape=[
            jax.ShapeDtypeStruct((seq_len, width), jnp.bfloat16),
            jax.ShapeDtypeStruct(cache.shape, jnp.bfloat16),
        ],
        compiler_params=pltpu.CompilerParams(
            dimension_semantics=("arbitrary",), vmem_limit_bytes=48 << 20
        ),
        interpret=interpret,
        name="attend",
    )(info, arrived, cache, sink, cosine, sine)


def pick_kernel(order, source, target):
    target[0] = source[order[pl.program_id(0)]]


def pick_rows(order, source):
    zeros = (0,) * (source.ndim - 1)
    return pl.pallas_call(
        pick_kernel,
        grid_spec=pltpu.PrefetchScalarGridSpec(
            num_scalar_prefetch=1,
            grid=(order.shape[0],),
            in_specs=[
                pl.BlockSpec(
                    source.shape, lambda i, order: (0,) + zeros, pipeline_mode=pl.Buffered(1)
                )
            ],
            out_specs=pl.BlockSpec((1,) + source.shape[1:], lambda i, order: (i,) + zeros),
        ),
        out_shape=jax.ShapeDtypeStruct((order.shape[0],) + source.shape[1:], source.dtype),
        compiler_params=pltpu.CompilerParams(dimension_semantics=("arbitrary",)),
        name="pick_rows",
    )(order, source)


def expert_kernel(
    rows, gate_a, up_a, down_a, gate_b, up_b, down_b, answer, gate_v, up_v, down_v, first, sems
):
    piece = pl.program_id(0)
    block = pl.program_id(1)
    size = rows.shape[0]
    sources = ((gate_a, up_a, down_a), (gate_b, up_b, down_b))

    def copies(number):
        targets = (gate_v.at[number], up_v.at[number], down_v.at[number])
        return [
            pltpu.make_async_copy(source, target, sems.at[number, index])
            for index, (source, target) in enumerate(zip(sources[number], targets))
        ]

    @pl.when((piece == 0) & (block == 0))
    def _():
        for copy in copies(0):
            copy.start()
        for copy in copies(0):
            copy.wait()
        for copy in copies(1):
            copy.start()

    @pl.when((piece == 1) & (block == 0))
    def _():
        for copy in copies(1):
            copy.wait()

    value = rows[...]
    contract_last = (((1,), (1,)), ((), ()))
    gate_part = lax.dot_general(
        value, gate_v[piece], contract_last, preferred_element_type=jnp.float32
    )
    up_part = lax.dot_general(value, up_v[piece], contract_last, preferred_element_type=jnp.float32)
    active = (jax.nn.silu(gate_part) * up_part).astype(jnp.bfloat16)
    output = jnp.dot(active, down_v[piece], preferred_element_type=jnp.float32).astype(jnp.bfloat16)
    at = pl.ds(pl.multiple_of(block * size, size), size)

    @pl.when(piece == 0)
    def _():
        first[at, :] = output

    @pl.when(piece == 1)
    def _():
        answer[...] = (first[at, :].astype(jnp.float32) + output.astype(jnp.float32)).astype(
            jnp.bfloat16
        )


def run_experts(rows, own, other, interpret=False):
    count, model_width = rows.shape
    units = own[0].shape[0]
    size = min(EXPERT_ROWS, count)
    anywhere = pl.BlockSpec(memory_space=pl.ANY)
    return pl.pallas_call(
        expert_kernel,
        grid=(SPLIT, count // size),
        in_specs=[pl.BlockSpec((size, model_width), lambda p, i: (i, 0))] + [anywhere] * 6,
        out_specs=pl.BlockSpec((size, model_width), lambda p, i: (p * i, 0)),
        out_shape=jax.ShapeDtypeStruct(rows.shape, jnp.bfloat16),
        scratch_shapes=[
            pltpu.VMEM((SPLIT, units, model_width), jnp.bfloat16),
            pltpu.VMEM((SPLIT, units, model_width), jnp.bfloat16),
            pltpu.VMEM((SPLIT, units, model_width), jnp.bfloat16),
            pltpu.VMEM(rows.shape, jnp.bfloat16),
            pltpu.SemaphoreType.DMA((SPLIT, 3)),
        ],
        compiler_params=pltpu.CompilerParams(
            dimension_semantics=("arbitrary", "arbitrary"), vmem_limit_bytes=56 << 20
        ),
        interpret=interpret,
        name="run_experts",
    )(rows, *own, *other)


def on_device(
    hidden,
    q_new,
    k_new,
    v_new,
    routes,
    slot_request,
    lengths,
    cycle_cache,
    sink_cache,
    w_out,
    norm_gain,
    router,
    w_gate,
    w_up,
    w_down,
):
    group_width = lax.axis_size("exp")
    group_count = lax.axis_size("req")
    devices_all = group_count * group_width
    group_index = lax.axis_index("req")
    member_index = lax.axis_index("exp")
    slots_here, local_rows, model_width = hidden.shape
    head_count = q_new.shape[1]
    head_dim = q_new.shape[3]
    experts_all = router.shape[1]
    slots_all = slot_request.shape[0]
    seq_len = local_rows * group_width
    tokens = slots_here * local_rows

    held = jnp.clip(slot_request - group_index * slots_here, 0, slots_here - 1)
    source_group = slot_request // slots_here

    def laid_out(part):
        chosen = part[0][None]
        for index in range(1, slots_here):
            flag = (held == index).reshape((slots_all,) + (1,) * (part.ndim - 1))
            chosen = jnp.where(flag, part[index][None], chosen)
        return chosen

    share = local_rows // group_count
    quarters = [
        part.reshape(slots_here, head_count, group_count, share, head_dim)
        for part in (q_new, k_new, v_new)
    ]
    outgoing = jnp.transpose(jnp.concatenate(quarters, axis=3), (2, 0, 1, 3, 4))
    spread = lax.all_to_all(outgoing, "req", split_axis=0, concat_axis=0, tiled=True)
    spread = spread.reshape(slots_all, head_count, 3 * share, head_dim)
    spread = pick_rows(slot_request, spread).reshape(devices_all, 3 * share, head_dim)
    arrived = lax.all_to_all(spread, ("req", "exp"), split_axis=0, concat_axis=0, tiled=True)
    arrived = arrived.reshape(group_count, group_width, 3 * share, head_dim)

    swap = [(index, index ^ 1) for index in range(group_width)]
    own_weights = (w_gate.T, w_up.T, w_down)
    other_weights = tuple(lax.ppermute(part, "exp", swap) for part in own_weights)

    slot_here = group_index * slots_here + member_index // head_count
    length = lax.dynamic_index_in_dim(lengths, slot_here, 0, keepdims=False)
    cosine, sine = rotary_tables(length, seq_len, head_dim)
    sink_count = sink_cache.shape[2]
    sink_padded = jnp.pad(sink_cache, ((0, 0), (0, 0), (0, SINK_PAD - sink_count), (0, 0)))
    info = jnp.stack([length, jnp.int32(sink_count)]).astype(jnp.int32)

    routes_wide = jnp.pad(
        routes.astype(jnp.bfloat16), ((0, 0), (0, 0), (0, 128 - routes.shape[2]))
    )
    states = laid_out(jnp.concatenate([hidden, routes_wide], axis=2))
    states = states.reshape(group_count, tokens, model_width + 128)
    states, arrived, cosine, sine, sink_padded, info, other_weights = lax.optimization_barrier(
        (states, arrived, cosine, sine, sink_padded, info, other_weights)
    )
    states = lax.all_to_all(states, "req", split_axis=0, concat_axis=0, tiled=True)

    def picked_states(states):
        states = states.reshape(group_count, slots_here, local_rows, model_width + 128)
        own_sources = lax.dynamic_slice_in_dim(
            source_group, group_index * slots_here, slots_here
        )
        states = jnp.concatenate(
            [
                lax.dynamic_index_in_dim(states[:, slot], own_sources[slot], 0, keepdims=False)
                for slot in range(slots_here)
            ],
            0,
        )
        hidden_sel = states[:, :model_width]
        route_sel = states[:, model_width : model_width + routes.shape[2]].astype(jnp.int32)
        return hidden_sel, route_sel

    context, cycle_out = attend(info, arrived, cycle_cache, sink_padded, cosine, sine)

    context, states = lax.optimization_barrier((context, states))
    hidden_sel, route_sel = picked_states(states)
    context_rows = lax.all_to_all(
        context.reshape(group_width, local_rows, head_dim),
        "exp",
        split_axis=0,
        concat_axis=0,
        tiled=True,
    ).reshape(slots_here, head_count, local_rows, head_dim)
    context_rows = jnp.transpose(context_rows, (0, 2, 1, 3)).reshape(tokens, head_count * head_dim)
    projected = jnp.dot(context_rows, w_out, preferred_element_type=jnp.float32)
    residual = hidden_sel.astype(jnp.float32) + projected
    inverse = lax.rsqrt(jnp.mean(residual * residual, axis=-1, keepdims=True) + 1e-06)
    normed = (residual * inverse * norm_gain).astype(jnp.bfloat16)

    logits = lax.dot_general(
        router, normed, (((0,), (1,)), ((), ())), preferred_element_type=jnp.float32
    )
    expert_ids = jnp.arange(experts_all, dtype=jnp.int32)
    named = jnp.any(route_sel.T[None] == expert_ids[:, None, None], axis=1)
    token_ids = jnp.arange(tokens, dtype=jnp.int32)
    token_slot = token_ids // local_rows
    before = (token_ids[:, None] < token_ids[None, :]) & (
        token_slot[:, None] == token_slot[None, :]
    )
    ranks = jnp.dot(
        named.astype(jnp.bfloat16), before.astype(jnp.bfloat16), preferred_element_type=jnp.float32
    ).astype(jnp.int32)
    masked = jnp.where(named, logits, -jnp.inf)
    raised = jnp.exp(masked - jnp.max(masked, axis=0, keepdims=True))
    gates = raised / jnp.sum(raised, axis=0, keepdims=True)
    per_chunk = slots_here // CHUNKS
    span = per_chunk * local_rows
    seats = jnp.arange(per_chunk * MOST, dtype=jnp.int32)
    wanted = (token_slot % per_chunk)[None, :] * MOST + ranks
    seated = named[:, None, :] & (wanted[:, None, :] == seats[None, :, None])
    shares = jnp.where(seated, gates[:, None, :], 0.0)
    seats_all = experts_all * per_chunk * MOST

    def exchanged(rows):
        return lax.all_to_all(
            rows.reshape(devices_all, seats_all // devices_all, model_width),
            ("req", "exp"),
            split_axis=0,
            concat_axis=0,
            tiled=True,
        ).reshape(seats_all, model_width)

    def slot_part(array, slot):
        return array[..., slot * span : (slot + 1) * span].reshape(seats_all, span)

    def dispatched(slot):
        return jnp.dot(
            slot_part(seated, slot).astype(jnp.bfloat16),
            normed[slot * span : (slot + 1) * span],
            preferred_element_type=jnp.float32,
        ).astype(jnp.bfloat16)

    def combined(slot, returned):
        part = slot_part(shares, slot)
        coarse = lax.reduce_precision(part, 8, 7)
        fine = (part - coarse).astype(jnp.bfloat16)
        both = jnp.concatenate([coarse.astype(jnp.bfloat16), fine], axis=1)
        moe = lax.dot_general(
            both, returned, (((0,), (0,)), ((), ())), preferred_element_type=jnp.float32
        )
        kept = residual[slot * span : (slot + 1) * span]
        return (kept + (moe[:span] + moe[span:])).astype(jnp.bfloat16)

    sent = [dispatched(slot) for slot in range(CHUNKS)]
    received = []
    for slot in range(CHUNKS):
        if slot:
            sent[slot], received[slot - 1] = lax.optimization_barrier(
                (sent[slot], received[slot - 1])
            )
        received.append(exchanged(sent[slot]))
    outputs = []
    for slot in range(CHUNKS):
        answer = run_experts(received[slot], own_weights, other_weights)
        if slot + 1 < CHUNKS:
            answer, received[CHUNKS - 1] = lax.optimization_barrier((answer, received[CHUNKS - 1]))
        outputs.append(exchanged(answer))
    layer_out = jnp.concatenate([combined(slot, outputs[slot]) for slot in range(CHUNKS)])
    layer_out = layer_out.reshape(slots_here, local_rows, model_width)
    return (layer_out, cycle_out)


def solution(mesh):
    in_specs = (
        P("req", "exp", None),
        P("req", None, "exp", None),
        P("req", None, "exp", None),
        P("req", None, "exp", None),
        P("req", "exp", None),
        P(),
        P(),
        P(("req", "exp"), None, None, None),
        P(("req", "exp"), None, None, None),
        P(),
        P(),
        P(),
        P(None, ("req", "exp")),
        P(None, ("req", "exp")),
        P(("req", "exp"), None),
    )
    out_specs = (P("req", "exp", None), P(("req", "exp"), None, None, None))

    return jax.shard_map(
        on_device, mesh=mesh, in_specs=in_specs, out_specs=out_specs, check_vma=False
    )
```
